512 devices in a mesh: patch: 64 (over x, z_hi, y, core), uly: 8 (over z_lo).
Axes of the slice: x: 4, y: 4, z: 16 (z_hi: 2, z_lo: 8; z = z_hi * 8 + z_lo), core: 2. Of those that a mesh axis runs over, the one named last changes fastest.
Arguments:
- queries: bfloat16 [8192, 3072], P(('patch', 'uly')), may hold values from -512 to 512
- keys_new: bfloat16 [8192, 3072], P(('patch', 'uly')), may hold values from -6 to 6
- values_new: bfloat16 [8192, 3072], P(('patch', 'uly')), may hold values from -6 to 6
- keys_old: bfloat16 [8192, 3072], P(('patch', 'uly')), may hold values from -8 to 8
- values_old: bfloat16 [8192, 3072], P(('patch', 'uly')), may hold values from -6 to 6
- gate_table: float32 [50, 3072], replicated, may hold values from 0.5 to 2
- step_index: int32 [1], replicated, may hold values from 0 to 49
Outputs:
- attended: bfloat16 [8192, 3072], P(('patch', 'uly'))
The draws below stay inside these ranges and needn't reach their ends.
All inputs are finite; a program needn't handle non-finite values.
Results may differ from the reference program's by a relative error of at most 0.0045.
Values may be sent and summed in bfloat16 or wider, within the bound.
A program may use at most 64 MiB of HBM per device.

```python
import math
import jax
import jax.numpy as jnp
from jax import lax

HEADS = 24
HEAD_DIM = 128
TOK_DEV = 16
STEPS = 50
D = 3072
TOKENS = 8192
N_PATCH = 64
N_ULY = 8


def shared_fields(key):
    query_key = jax.random.fold_in(key, 11)
    stale_key = jax.random.fold_in(key, 23)
    query_field = jnp.clip(3.0 * jax.random.normal(query_key, (TOKENS, D), jnp.float32), -18.0, 18.0)
    stale_field = jnp.clip(jax.random.normal(stale_key, (TOKENS, D), jnp.float32), -6.0, 6.0)
    return (query_field, stale_field)


def draw_queries(key, part):
    return shared_fields(key)[0].astype(jnp.bfloat16)


def draw_keys_old(key, part):
    return shared_fields(key)[1].astype(jnp.bfloat16)


def levels(key, extent, shards, smallest, high):
    factor_of, own = 1.0, jax.random.fold_in(key, 6)
    for axis_at, blocks in shards:
        steps = jnp.exp(jax.random.uniform(jax.random.fold_in(own, axis_at), (blocks,), jnp.float32, smallest / len(shards), high / len(shards)))
        factor_of = factor_of * jnp.repeat(steps, extent[axis_at] // blocks).reshape([-1 if axis == axis_at else 1 for axis in range(len(extent))])
    return factor_of


def scatter_about(key, extent, deviation, bound, split=(), held_as=jnp.bfloat16):
    entries = jax.random.normal(key, extent, jnp.float32) * deviation
    if len(split) > 0:
        entries = levels(key, extent, split, -0.22, 0.18) * entries
    return jnp.clip(entries, min=-bound, max=bound).astype(held_as)


def setup_inputs(seed: int = 0) -> dict:
    streams_of = jax.random.split(jax.random.key(seed), 8)
    queries = draw_queries(jax.random.fold_in(streams_of[7], 71), 0)
    keys_new = scatter_about(streams_of[1], (TOKENS, D), 1.0, 6.0, ((0, 512),))
    values_new = scatter_about(streams_of[2], (TOKENS, D), 1.0, 6.0, ((0, 512),))
    keys_old = draw_keys_old(jax.random.fold_in(streams_of[7], 71), 0)
    values_old = scatter_about(streams_of[4], (TOKENS, D), 1.0, 6.0, ((0, 512),))
    gate_table = jnp.clip(jnp.exp(jax.random.uniform(streams_of[5], (STEPS, D), jnp.float32, math.log(0.5), math.log(2.0))), 0.5, 2.0)
    step_index = jax.random.randint(streams_of[6], (1,), 0, STEPS).astype(jnp.int32)
    return dict(queries=queries, keys_new=keys_new, values_new=values_new, keys_old=keys_old, values_old=values_old, gate_table=gate_table, step_index=step_index)


def reference(queries, keys_new, values_new, keys_old, values_old, gate_table, step_index):
    rows = TOK_DEV * N_ULY
    total_rows = rows * N_PATCH
    scale = HEAD_DIM ** -0.5
    picker = (jnp.arange(STEPS, dtype=jnp.int32) == step_index[0]).astype(jnp.float32)
    gate = jnp.dot(picker, gate_table, precision=lax.Precision.HIGHEST)
    old_keys = keys_old.astype(jnp.float32).reshape(total_rows, HEADS, HEAD_DIM)
    old_values = values_old.astype(jnp.float32).reshape(total_rows, HEADS, HEAD_DIM)
    positions = jnp.arange(total_rows, dtype=jnp.int32)

    def one_patch(patch_id):
        start = (patch_id * rows).astype(jnp.int32)
        query_block = lax.dynamic_slice_in_dim(queries, start, rows, 0).astype(jnp.float32).reshape(rows, HEADS, HEAD_DIM)
        key_block = lax.dynamic_slice_in_dim(keys_new, start, rows, 0).astype(jnp.float32).reshape(rows, HEADS, HEAD_DIM)
        value_block = lax.dynamic_slice_in_dim(values_new, start, rows, 0).astype(jnp.float32).reshape(rows, HEADS, HEAD_DIM)
        score_old = jnp.einsum("phd,khd->hpk", query_block, old_keys) * scale
        score_new = jnp.einsum("phd,khd->hpk", query_block, key_block) * scale
        own = (positions // rows) == patch_id
        score_old = jnp.where(own[None, None, :], jnp.float32(-1e30), score_old)
        rowmax = jnp.maximum(jnp.max(score_old, axis=-1), jnp.max(score_new, axis=-1))
        expo_old = jnp.exp(score_old - rowmax[..., None])
        expo_new = jnp.exp(score_new - rowmax[..., None])
        total = jnp.sum(expo_old, axis=-1) + jnp.sum(expo_new, axis=-1)
        weight_old = lax.optimization_barrier(expo_old.astype(jnp.bfloat16)).astype(jnp.float32)
        weight_new = lax.optimization_barrier(expo_new.astype(jnp.bfloat16)).astype(jnp.float32)
        summed = jnp.einsum("hpk,khd->phd", weight_old, old_values) + jnp.einsum("hpk,khd->phd", weight_new, value_block)
        mixed = summed / jnp.transpose(total)[..., None]
        return (mixed.reshape(rows, HEADS * HEAD_DIM) * gate).astype(jnp.bfloat16)

    blocks = lax.map(one_patch, jnp.arange(N_PATCH, dtype=jnp.int32))
    return blocks.reshape(total_rows, HEADS * HEAD_DIM)
```

```python
import jax
import jax.numpy as jnp
from jax import lax
from jax.experimental import pallas as pl
from jax.experimental.pallas import tpu as pltpu
from jax.sharding import PartitionSpec as P

HEADS = 24
HEAD_DIM = 128
MESH = pl.DeviceIdType.MESH
TOK = 16
RING = 16
SIDE = 4
C = HEAD_DIM ** (-0.5) * 1.4426950408889634

ORDER = (
    (0, 0), (1, 0), (3, 0), (0, 1), (0, 3), (2, 0), (1, 1), (1, 3),
    (3, 1), (3, 3), (0, 2), (2, 1), (2, 3), (1, 2), (3, 2), (2, 2),
)
SLOT = {pair: at for at, pair in enumerate(ORDER)}
OWN_STEP = 8


def kernel(
    q_in, kn_in, vn_in, ko_in, vo_in, gate_in, step_ref, out_ref,
    stage, gbuf, kv, qa, acc, mx, tot, stat, racc, rstat, obuf, outbuf,
    stage_sem, gate_sem, kv_send, kv_recv, q_send, q_recv, qf_send, qf_recv,
    new_send, new_recv, old_sem, xy_send, xy_recv, part_send, part_recv, out_send, out_recv,
):
    p = lax.axis_index("patch")
    zl = lax.axis_index("uly")
    c = lax.rem(p, 2)
    y = lax.rem(p // 2, SIDE)
    zh = lax.rem(p // 8, 2)
    x = p // 16
    z = zh * 8 + zl
    g, s = z // 2, lax.rem(z, 2)

    def patch_of(x_, zh_, y_, c_):
        return ((x_ * 2 + zh_) * SIDE + y_) * 2 + c_

    def z_dev(z_):
        return {"patch": patch_of(x, z_ // 8, y, c), "uly": lax.rem(z_, 8)}

    def xy_dev(da, db):
        x_ = lax.rem(x + da * (1 - c) + db * c, SIDE)
        y_ = lax.rem(y + da * c + db * (1 - c), SIDE)
        return {"patch": patch_of(x_, zh, y_, c), "uly": zl}

    partner = {"patch": patch_of(x, zh, y, 1 - c), "uly": zl}

    def lanes(at, n=HEAD_DIM):
        return pl.ds(pl.multiple_of(at, HEAD_DIM), n)

    def rows(at, n):
        return pl.ds(pl.multiple_of(at, TOK), n)

    def remote(src, dst, ssem, rsem, dev):
        return pltpu.make_async_remote_copy(
            src_ref=src, dst_ref=dst, send_sem=ssem, recv_sem=rsem, device_id=dev, device_id_type=MESH
        )

    col = lanes((3 * g + s) * HEAD_DIM, 256)
    loads = [
        pltpu.make_async_copy(ref, stage.at[at], stage_sem.at[at])
        for at, ref in enumerate((ko_in, vo_in, q_in, kn_in, vn_in))
    ]
    for load in loads:
        load.start()
    gate_load = pltpu.make_async_copy(gate_in.at[:, col], gbuf, gate_sem)
    gate_load.start()

    barrier = pltpu.get_barrier_semaphore()

    def greet(d, carry):
        pl.semaphore_signal(barrier, inc=1, device_id=z_dev(lax.rem(z + d, RING)), device_id_type=MESH)
        return carry

    lax.fori_loop(1, RING, greet, 0)
    for da, db in ((1, 0), (3, 0), (0, 1), (0, 3)):
        pl.semaphore_signal(barrier, inc=1, device_id=xy_dev(da, db), device_id_type=MESH)
    pl.semaphore_signal(barrier, inc=1, device_id=partner, device_id_type=MESH)
    acc[...] = jnp.zeros_like(acc)
    tot[...] = jnp.zeros_like(tot)
    mx[...] = jnp.full_like(mx, -1e30)
    for load in loads:
        load.wait()
    pl.semaphore_wait(barrier, RING - 1 + 4 + 1)

    mine = rows(z * TOK, TOK)
    here = rows(zl * TOK, TOK)

    def far(i):
        return lax.rem(z + 8 + ((i + 1) // 2) * (2 * lax.rem(i, 2) - 1), RING)

    def two_heads(z_):
        return lanes((3 * (z_ // 2) + lax.rem(z_, 2)) * HEAD_DIM, 256)

    def main_head(z_):
        return lanes((3 * (z_ // 2) + 2 * lax.rem(z_, 2)) * HEAD_DIM)

    def send_kv(i, carry):
        t = far(i)
        for at in range(2):
            remote(
                stage.at[at, :, two_heads(t)], kv.at[0, mine, 256 * at:256 * at + 256],
                kv_send, kv_recv, z_dev(t),
            ).start()
        return carry

    lax.fori_loop(0, RING - 1, send_kv, 0)
    for at in range(2):
        pltpu.make_async_copy(
            stage.at[at, :, two_heads(z)], kv.at[0, mine, 256 * at:256 * at + 256], kv_recv
        ).start()

    def send_q(i, carry):
        t = far(i)

        @pl.when(lax.rem(t, 2) == zh)
        def _():
            remote(stage.at[2, :, two_heads(t)], qa.at[c, mine, :], q_send, q_recv, z_dev(t)).start()

        @pl.when(lax.rem(t, 2) != zh)
        def _():
            remote(
                stage.at[2, :, main_head(t)], qa.at[c, mine, lanes(lax.rem(t, 2) * HEAD_DIM)],
                q_send, q_recv, z_dev(t),
            ).start()

        return carry

    lax.fori_loop(0, RING - 1, send_q, 0)

    def send_new(i, carry):
        t = far(i)

        @pl.when(lax.rem(t, 2) == zh)
        def _():
            for at in range(2):
                remote(
                    stage.at[3 + at, :, two_heads(t)], kv.at[RING + zh, mine, 256 * at:256 * at + 256],
                    new_send, new_recv, z_dev(t),
                ).start()

        @pl.when(lax.rem(t, 2) != zh)
        def _():
            for at in range(2):
                remote(
                    stage.at[3 + at, :, main_head(t)],
                    kv.at[RING + zh, mine, lanes(256 * at + lax.rem(t, 2) * HEAD_DIM)],
                    new_send, new_recv, z_dev(t),
                ).start()

        return carry

    lax.fori_loop(0, RING - 1, send_new, 0)

    @pl.when(s == zh)
    def _():
        pltpu.make_async_copy(stage.at[2, :, two_heads(z)], qa.at[c, mine, :], q_recv).start()
        for at in range(2):
            pltpu.make_async_copy(
                stage.at[3 + at, :, two_heads(z)], kv.at[RING + zh, mine, 256 * at:256 * at + 256], new_recv
            ).start()

    @pl.when(s != zh)
    def _():
        pltpu.make_async_copy(
            stage.at[2, :, main_head(z)], qa.at[c, mine, lanes(s * HEAD_DIM)], q_recv
        ).start()
        for at in range(2):
            pltpu.make_async_copy(
                stage.at[3 + at, :, main_head(z)],
                kv.at[RING + zh, mine, lanes(256 * at + s * HEAD_DIM)], new_recv,
            ).start()

    half_rows = (slice(0, 128), slice(128, 256))

    def push(src, dst, da, db, part=None):
        a, b = kv.at[SLOT[src]], kv.at[SLOT[dst]]
        if part is not None:
            a, b = kv.at[SLOT[src], half_rows[part]], kv.at[SLOT[dst], half_rows[part]]
        remote(a, b, xy_send, xy_recv.at[SLOT[dst]], xy_dev(da, db)).start()

    def pass_on(pair):
        da, db = pair
        if pair == (0, 0):
            push(pair, (1, 0), 1, 0)
            push(pair, (3, 0), 3, 0)
        if pair == (1, 0):
            push(pair, (2, 0), 1, 0, 0)
        if pair == (3, 0):
            push(pair, (2, 0), 3, 0, 1)
        if db == 0:
            push(pair, (da, 1), 0, 1)
            push(pair, (da, 3), 0, 3)
        if db == 1:
            push(pair, (da, 2), 0, 1, 0)
        if db == 3:
            push(pair, (da, 2), 0, 3, 1)

    pltpu.make_async_copy(kv.at[0], kv.at[0], kv_recv).wait()
    pass_on((0, 0))
    for side in range(2):
        keep = half_rows[1 - side]
        pltpu.make_async_copy(kv.at[0, keep], kv.at[RING + side, keep], old_sem.at[side]).start()

    pltpu.make_async_copy(qa.at[c, 0:192], qa.at[c, 0:192], q_recv).wait()
    main_col, shared_col = lanes(s * HEAD_DIM), lanes((1 - s) * HEAD_DIM)
    shared_rows = rows(s * 128, 128)
    q_main = remote(
        qa.at[c, :, main_col], qa.at[c, :, main_col], qf_send.at[0], qf_recv.at[0], partner
    )
    q_shared = remote(
        qa.at[c, shared_rows, shared_col], qa.at[c, shared_rows, shared_col],
        qf_send.at[1], qf_recv.at[1], partner,
    )
    q_main.start()
    q_shared.start()
    q_main.wait()
    q_shared.wait()

    def absorb(core, at, count, queries, keys, values):
        dots = lax.dot_general(queries, keys, (((1,), (1,)), ((), ())), preferred_element_type=jnp.float32)
        there = (core, pl.ds(at, count))
        old = mx[there]
        new = jnp.maximum(old, jnp.max(dots, axis=1, keepdims=True))
        shrink = jnp.exp2((old - new) * C)
        expo = jnp.exp2((dots - new[:, :1]) * C)
        tot[there] = tot[there] * shrink + jnp.sum(expo, axis=1, keepdims=True)
        acc[there] = acc[there] * shrink + jnp.dot(
            expo.astype(jnp.bfloat16), values, preferred_element_type=jnp.float32
        )
        mx[there] = new

    main_val, shared_val = lanes(256 + s * HEAD_DIM), lanes(256 + (1 - s) * HEAD_DIM)

    def chunk(core, at):
        absorb(core, 0, 256, qa[core, :, main_col], kv[at, :, main_col], kv[at, :, main_val])
        absorb(
            core, 256, 128, qa[core, shared_rows, shared_col], kv[at, :, shared_col], kv[at, :, shared_val]
        )

    def own():
        pltpu.make_async_copy(kv.at[RING, 0:192], kv.at[RING, 0:192], new_recv).wait()
        for side in range(2):
            keep = half_rows[1 - side]
            pltpu.make_async_copy(kv.at[0, keep], kv.at[RING + side, keep], old_sem.at[side]).wait()
        chunk(1 - c, 0)
        for side in range(2):
            at = RING + side
            absorb(
                c, side * 128, 128, qa[c, half_rows[side], main_col], kv[at, :, main_col], kv[at, :, main_val]
            )
        at = RING + s
        absorb(c, 256, 128, qa[c, shared_rows, shared_col], kv[at, :, shared_col], kv[at, :, shared_val])

    partial = [
        remote(acc.at[1 - c], racc, part_send.at[0], part_recv.at[0], partner),
        remote(stat, rstat, part_send.at[1], part_recv.at[1], partner),
    ]

    def one_slot(k, carry):
        pltpu.make_async_copy(kv.at[k], kv.at[k], xy_recv.at[k]).wait()
        for at, pair in enumerate(ORDER):
            if at > 0 and pair[1] != 2:
                @pl.when(k == at)
                def _(pair=pair):
                    pass_on(pair)

        @pl.when(k == OWN_STEP)
        def _():
            own()

        chunk(1 - c, k)

        @pl.when(k == RING - 1)
        def _():
            low = lax.broadcasted_iota(jnp.int32, stat.shape, 1) < 64
            stat[...] = jnp.where(low, mx[1 - c], tot[1 - c])
            for copy in partial:
                copy.start()

        chunk(c, k)
        return carry

    lax.fori_loop(1, RING, one_slot, 0)

    gate_load.wait()
    picked = lax.broadcasted_iota(jnp.int32, gbuf.shape, 0) == step_ref[0]
    gate = jnp.sum(jnp.where(picked, gbuf[...], 0.0), axis=0, keepdims=True)
    gate_lo, gate_hi = gate[:, :HEAD_DIM], gate[:, HEAD_DIM:]
    gate_main = jnp.where(s == 0, gate_lo, gate_hi)
    gate_shared = jnp.where(s == 0, gate_hi, gate_lo)
    for copy in partial:
        copy.wait()
    for at, count, gated in ((0, 256, gate_main), (256, 128, gate_shared)):
        there = pl.ds(at, count)
        m1, m2 = mx[c, there], jnp.broadcast_to(rstat[there, 0:1], (count, HEAD_DIM))
        l2 = jnp.broadcast_to(rstat[there, 64:65], (count, HEAD_DIM))
        top = jnp.maximum(m1, m2)
        w1, w2 = jnp.exp2((m1 - top) * C), jnp.exp2((m2 - top) * C)
        mixed = (acc[c, there] * w1 + racc[there] * w2) / (tot[c, there] * w1 + l2 * w2)
        obuf[there] = (mixed * gated).astype(jnp.bfloat16)

    my_main, my_shared = main_head(z), lanes((3 * g + 1) * HEAD_DIM)

    def send_out(i, carry):
        t = far(i)
        remote(obuf.at[rows(t * TOK, TOK)], outbuf.at[:, my_main], out_send, out_recv, z_dev(t)).start()

        @pl.when(t // 8 == s)
        def _():
            remote(
                obuf.at[rows(256 + lax.rem(t, 8) * TOK, TOK)], outbuf.at[:, my_shared],
                out_send, out_recv, z_dev(t),
            ).start()

        return carry

    lax.fori_loop(0, RING - 1, send_out, 0)
    pltpu.make_async_copy(obuf.at[mine], outbuf.at[:, my_main], out_recv).start()

    @pl.when(zh == s)
    def _():
        pltpu.make_async_copy(
            obuf.at[rows(256 + zl * TOK, TOK)], outbuf.at[:, my_shared], out_recv
        ).start()

    def sent(ref, sem):
        pltpu.make_async_copy(ref, ref, sem).wait()

    sent(kv.at[0, 0:240], kv_send)
    sent(kv.at[pl.ds(1, 15)], xy_send)

    @pl.when(zh == s)
    def _():
        sent(qa.at[0, 0:176], q_send)
        sent(kv.at[RING, 0:176], new_send)
        sent(obuf.at[pl.ds(0, 22 * TOK)], out_send)

    @pl.when(zh != s)
    def _():
        sent(qa.at[0, 0:184], q_send)
        sent(kv.at[RING, 0:184], new_send)
        sent(obuf.at[pl.ds(0, 23 * TOK)], out_send)

    pltpu.make_async_copy(outbuf, outbuf, out_recv).wait()
    out_ref[...] = outbuf[...]


def body(queries, keys_new, values_new, keys_old, values_old, gate_table, step_index):
    bf, f32 = jnp.bfloat16, jnp.float32
    dma = pltpu.SemaphoreType.DMA
    return pl.pallas_call(
        kernel,
        out_shape=jax.ShapeDtypeStruct(queries.shape, bf),
        in_specs=[pl.BlockSpec(memory_space=pl.ANY)] * 6 + [pl.BlockSpec(memory_space=pltpu.SMEM)],
        out_specs=pl.BlockSpec(memory_space=pltpu.VMEM),
        scratch_shapes=[
            pltpu.VMEM((5, TOK, HEADS * HEAD_DIM), bf),
            pltpu.VMEM((gate_table.shape[0], 256), f32),
            pltpu.VMEM((RING + 2, 256, 512), bf),
            pltpu.VMEM((2, 256, 256), bf),
            pltpu.VMEM((2, 384, HEAD_DIM), f32),
            pltpu.VMEM((2, 384, HEAD_DIM), f32),
            pltpu.VMEM((2, 384, HEAD_DIM), f32),
            pltpu.VMEM((384, HEAD_DIM), f32),
            pltpu.VMEM((384, HEAD_DIM), f32),
            pltpu.VMEM((384, HEAD_DIM), f32),
            pltpu.VMEM((384, HEAD_DIM), bf),
            pltpu.VMEM((TOK, HEADS * HEAD_DIM), bf),
            dma((5,)), dma, dma, dma, dma, dma, dma((2,)), dma((2,)),
            dma, dma, dma((2,)), dma, dma((RING,)), dma((2,)), dma((2,)), dma, dma,
        ],
        compiler_params=pltpu.CompilerParams(collective_id=0, has_side_effects=True),
    )(queries, keys_new, values_new, keys_old, values_old, gate_table, step_index)


def solution(mesh):
    tokens = P(("patch", "uly"), None)
    return jax.shard_map(
        body, mesh=mesh, in_specs=(tokens,) * 5 + (P(), P()), out_specs=tokens, check_vma=False
    )
```

```python
import jax
import jax.numpy as jnp
from jax import lax
from jax.experimental import pallas as pl
from jax.experimental.pallas import tpu as pltpu
from jax.sharding import PartitionSpec as P

HEADS = 24
HEAD_DIM = 128
MESH = pl.DeviceIdType.MESH
TOK = 16
RING = 16
SIDE = 4
C = HEAD_DIM ** (-0.5) * 1.4426950408889634

ORDER = (
    (0, 0), (1, 0), (3, 0), (0, 1), (0, 3), (2, 0), (1, 1), (1, 3),
    (3, 1), (3, 3), (0, 2), (2, 1), (2, 3), (1, 2), (3, 2), (2, 2),
)
SLOT = {pair: at for at, pair in enumerate(ORDER)}
HALF = (slice(0, 128), slice(128, 256))
MAIN, SHARED = 0, 1
OTHER, OWN = 0, 1
AHEAD, EVEN = 3, 6
OWN_STEP = 11


def kernel(
    q_in, kn_in, vn_in, ko_in, vo_in, gate_in, step_ref, out_ref,
    raw, pairs, gbuf, kv, qa, acc_m, acc_s, st_m, st_s, racc_m, racc_s, rst_m, rst_s, obuf, outbuf,
    stage_sem, gate_sem, kv_send, kv_recv, q_send, q_recv, qf_send, qf_recv,
    new_send, new_recv, old_sem, xy_send, xy_recv, part_send, part_recv, out_send, out_recv,
):
    p = lax.axis_index("patch")
    zl = lax.axis_index("uly")
    c = lax.rem(p, 2)
    y = lax.rem(p // 2, SIDE)
    zh = lax.rem(p // 8, 2)
    x = p // 16
    z = zh * 8 + zl
    g, s = z // 2, lax.rem(z, 2)

    def patch_of(x_, zh_, y_, c_):
        return ((x_ * 2 + zh_) * SIDE + y_) * 2 + c_

    def z_dev(z_):
        return {"patch": patch_of(x, z_ // 8, y, c), "uly": lax.rem(z_, 8)}

    def xy_dev(da, db):
        x_ = lax.rem(x + da * (1 - c) + db * c, SIDE)
        y_ = lax.rem(y + da * c + db * (1 - c), SIDE)
        return {"patch": patch_of(x_, zh, y_, c), "uly": zl}

    partner = {"patch": patch_of(x, zh, y, 1 - c), "uly": zl}

    def lanes(at, n=HEAD_DIM):
        return pl.ds(pl.multiple_of(at, HEAD_DIM), n)

    def rows(at, n):
        return pl.ds(pl.multiple_of(at, TOK), n)

    def remote(src, dst, ssem, rsem, dev):
        return pltpu.make_async_remote_copy(
            src_ref=src, dst_ref=dst, send_sem=ssem, recv_sem=rsem, device_id=dev, device_id_type=MESH
        )

    loads = [
        pltpu.make_async_copy(ref, raw.at[at], stage_sem.at[at])
        for at, ref in enumerate((ko_in, vo_in, kn_in, vn_in, q_in))
    ]
    for load in loads:
        load.start()
    gate_load = pltpu.make_async_copy(gate_in.at[:, lanes((3 * g + s) * HEAD_DIM, 256)], gbuf, gate_sem)
    gate_load.start()

    barrier = pltpu.get_barrier_semaphore()

    def greet(d, carry):
        pl.semaphore_signal(barrier, inc=1, device_id=z_dev(lax.rem(z + d, RING)), device_id_type=MESH)
        return carry

    lax.fori_loop(1, RING, greet, 0)
    for da, db in ((1, 0), (3, 0), (0, 1), (0, 3)):
        pl.semaphore_signal(barrier, inc=1, device_id=xy_dev(da, db), device_id_type=MESH)
    pl.semaphore_signal(barrier, inc=1, device_id=partner, device_id_type=MESH)
    for ref in (acc_m, acc_s):
        ref[...] = jnp.zeros_like(ref)
    for ref in (st_m, st_s):
        at = lax.broadcasted_iota(jnp.int32, ref.shape, 1)
        ref[...] = jnp.where(at == 0, -1e30, 0.0)
    for load in loads:
        load.wait()
    for at in range(4):
        for head in range(HEADS):
            col = (2 * head + at % 2) * HEAD_DIM
            pairs[at // 2, :, col:col + HEAD_DIM] = raw[at, :, head * HEAD_DIM:(head + 1) * HEAD_DIM]
    pl.semaphore_wait(barrier, RING - 1 + 4 + 1)

    mine = rows(z * TOK, TOK)

    def far(i):
        return lax.rem(z + 8 + ((i + 1) // 2) * (2 * lax.rem(i, 2) - 1), RING)

    def head_of(z_, which):
        group = 3 * (z_ // 2)
        return group + 1 if which == SHARED else group + 2 * lax.rem(z_, 2)

    def pair_of(z_, which):
        return lanes(256 * head_of(z_, which), 256)

    def single_of(z_, which):
        return lanes(HEAD_DIM * head_of(z_, which))

    def to_all(one):
        def step(i, carry):
            one(far(i))
            return carry

        lax.fori_loop(0, RING - 1, step, 0)

    def send_old(which):
        to_all(lambda t: remote(
            pairs.at[0, :, pair_of(t, which)], kv.at[which, 0, mine, :],
            kv_send.at[which], kv_recv.at[which], z_dev(t),
        ).start())
        pltpu.make_async_copy(
            pairs.at[0, :, pair_of(z, which)], kv.at[which, 0, mine, :], kv_recv.at[which]
        ).start()

    q_cols = (slice(0, 128), slice(128, 256))

    def send_q(t):
        remote(
            raw.at[4, :, single_of(t, MAIN)], qa.at[OWN, mine, q_cols[MAIN]], q_send, q_recv, z_dev(t)
        ).start()

        @pl.when(lax.rem(t, 2) == zh)
        def _():
            remote(
                raw.at[4, :, single_of(t, SHARED)], qa.at[OWN, mine, q_cols[SHARED]], q_send, q_recv, z_dev(t)
            ).start()

    def send_new(t):
        remote(
            pairs.at[1, :, pair_of(t, MAIN)], kv.at[MAIN, RING + zh, mine, :],
            new_send, new_recv.at[MAIN], z_dev(t),
        ).start()

    def send_new_shared(t):
        @pl.when(lax.rem(t, 2) == zh)
        def _():
            remote(
                pairs.at[1, :, pair_of(t, SHARED)], kv.at[SHARED, RING + zh, mine, :],
                new_send, new_recv.at[SHARED], z_dev(t),
            ).start()

    send_old(MAIN)
    send_old(SHARED)

    def start_queries():
        to_all(send_q)
        pltpu.make_async_copy(raw.at[4, :, single_of(z, MAIN)], qa.at[OWN, mine, q_cols[MAIN]], q_recv).start()

        @pl.when(s == zh)
        def _():
            pltpu.make_async_copy(
                raw.at[4, :, single_of(z, SHARED)], qa.at[OWN, mine, q_cols[SHARED]], q_recv
            ).start()

    def start_new():
        to_all(send_new)
        pltpu.make_async_copy(
            pairs.at[1, :, pair_of(z, MAIN)], kv.at[MAIN, RING + zh, mine, :], new_recv.at[MAIN]
        ).start()
        to_all(send_new_shared)

        @pl.when(s == zh)
        def _():
            pltpu.make_async_copy(
                pairs.at[1, :, pair_of(z, SHARED)], kv.at[SHARED, RING + zh, mine, :], new_recv.at[SHARED]
            ).start()


    def push(which, src, dst, da, db, part=None):
        a, b = kv.at[which, SLOT[src]], kv.at[which, SLOT[dst]]
        if part is not None:
            a, b = kv.at[which, SLOT[src], HALF[part]], kv.at[which, SLOT[dst], HALF[part]]
        remote(a, b, xy_send, xy_recv.at[which, SLOT[dst]], xy_dev(da, db)).start()

    def pass_on(which, pair):
        da, db = pair
        if pair == (0, 0):
            push(which, pair, (1, 0), 1, 0)
            push(which, pair, (3, 0), 3, 0)
        if pair == (1, 0):
            push(which, pair, (2, 0), 1, 0, 0)
        if pair == (3, 0):
            push(which, pair, (2, 0), 3, 0, 1)
        if db == 0:
            push(which, pair, (da, 1), 0, 1)
            push(which, pair, (da, 3), 0, 3)
        if db == 1:
            push(which, pair, (da, 2), 0, 1, 0)
        if db == 3:
            push(which, pair, (da, 2), 0, 3, 1)

    def begin(which):
        whole = kv.at[which, 0]
        pltpu.make_async_copy(whole, whole, kv_recv.at[which]).wait()
        pass_on(which, (0, 0))
        for side in range(2):
            keep = HALF[1 - side]
            pltpu.make_async_copy(
                kv.at[which, 0, keep], kv.at[which, RING + side, keep], old_sem.at[which, side]
            ).start()

    def arrived(which, k):
        pltpu.make_async_copy(kv.at[which, k], kv.at[which, k], xy_recv.at[which, k]).wait()

    def take(k, first, last):
        for which in range(2):
            arrived(which, k)
            for at in range(first, last):
                if ORDER[at][1] != 2:
                    @pl.when(k == at)
                    def _(pair=ORDER[at]):
                        pass_on(which, pair)

    begin(MAIN)
    begin(SHARED)
    start_queries()
    start_new()
    for k in range(1, AHEAD + 1):
        for which in range(2):
            arrived(which, k)
            pass_on(which, ORDER[k])

    pltpu.make_async_copy(qa.at[OWN, 0:192], qa.at[OWN, 0:192], q_recv).wait()
    shared_rows = rows(s * 128, 128)
    q_main = remote(
        qa.at[OWN, :, q_cols[MAIN]], qa.at[OTHER, :, q_cols[MAIN]], qf_send.at[0], qf_recv.at[0], partner
    )
    q_shared = remote(
        qa.at[OWN, shared_rows, q_cols[SHARED]], qa.at[OTHER, shared_rows, q_cols[SHARED]],
        qf_send.at[1], qf_recv.at[1], partner,
    )
    q_main.start()
    q_shared.start()
    q_main.wait()
    q_shared.wait()

    def absorb(acc, st, core, across, queries, block):
        keys, values = block[:, :HEAD_DIM], block[:, HEAD_DIM:]
        dots = lax.dot_general(keys, queries, (((1,), (1,)), ((), ())), preferred_element_type=jnp.float32)
        old = st[core, 0:1, across]
        new = jnp.maximum(old, jnp.max(dots, axis=0, keepdims=True))
        shrink = jnp.exp2((old - new) * C)
        expo = jnp.exp2((dots - new) * C)
        st[core, 1:2, across] = st[core, 1:2, across] * shrink + jnp.sum(expo, axis=0, keepdims=True)
        acc[core, :, across] = acc[core, :, across] * shrink + lax.dot_general(
            values, expo.astype(jnp.bfloat16), (((0,), (0,)), ((), ())), preferred_element_type=jnp.float32
        )
        st[core, 0:1, across] = new

    def main_chunk(core, k):
        absorb(acc_m, st_m, core, slice(0, 256), qa[core, :, q_cols[MAIN]], kv.at[MAIN, k])

    def shared_chunk(core, k):
        absorb(acc_s, st_s, core, slice(0, 128), qa[core, shared_rows, q_cols[SHARED]], kv.at[SHARED, k])

    def whole(k):
        jobs = [
            (acc, st, core, queries, kv.at[which, k])
            for core in (OTHER, OWN)
            for acc, st, which, queries in (
                (acc_m, st_m, MAIN, qa[core, :, q_cols[MAIN]]),
                (acc_s, st_s, SHARED, qa[core, shared_rows, q_cols[SHARED]]),
            )
        ]
        scored, mixed = [], []
        for acc, st, core, queries, block in jobs:
            dots = lax.dot_general(
                block[:, :HEAD_DIM], queries, (((1,), (1,)), ((), ())), preferred_element_type=jnp.float32
            )
            scored.append((dots, jnp.maximum(st[core, 0:1], jnp.max(dots, axis=0, keepdims=True))))
        for (acc, st, core, queries, block), (dots, new) in zip(jobs, scored):
            expo = jnp.exp2((dots - new) * C)
            shrink = jnp.exp2((st[core, 0:1] - new) * C)
            mixed.append((shrink, jnp.sum(expo, axis=0, keepdims=True), lax.dot_general(
                block[:, HEAD_DIM:], expo.astype(jnp.bfloat16), (((0,), (0,)), ((), ())),
                preferred_element_type=jnp.float32,
            )))
        for (acc, st, core, queries, block), (dots, new), (shrink, added, update) in zip(jobs, scored, mixed):
            st[core, 1:2] = st[core, 1:2] * shrink + added
            acc[core] = acc[core] * shrink + update
            st[core, 0:1] = new

    def own_ready(which, count):
        got = kv.at[which, RING, 0:count]
        pltpu.make_async_copy(got, got, new_recv.at[which]).wait()
        for side in range(2):
            keep = HALF[1 - side]
            pltpu.make_async_copy(
                kv.at[which, 0, keep], kv.at[which, RING + side, keep], old_sem.at[which, side]
            ).wait()

    def partial(which):
        acc, st, racc, rst = ((acc_m, st_m, racc_m, rst_m), (acc_s, st_s, racc_s, rst_s))[which]
        return [
            remote(acc.at[OTHER], racc, part_send.at[which, 0], part_recv.at[which, 0], partner),
            remote(st.at[OTHER], rst, part_send.at[which, 1], part_recv.at[which, 1], partner),
        ]

    gate_load.wait()
    picked = lax.broadcasted_iota(jnp.int32, gbuf.shape, 0) == step_ref[0]
    gate = jnp.sum(jnp.where(picked, gbuf[...], 0.0), axis=0, keepdims=True)
    gate_lo, gate_hi = gate[:, :HEAD_DIM], gate[:, HEAD_DIM:]
    gates = (jnp.where(s == 0, gate_lo, gate_hi), jnp.where(s == 0, gate_hi, gate_lo))

    def merge(which):
        acc, st, racc, rst = ((acc_m, st_m, racc_m, rst_m), (acc_s, st_s, racc_s, rst_s))[which]
        for copy in partial(which):
            copy.wait()
        m1, l1, m2, l2 = st[OWN, 0:1], st[OWN, 1:2], rst[0:1], rst[1:2]
        top = jnp.maximum(m1, m2)
        w1, w2 = jnp.exp2((m1 - top) * C), jnp.exp2((m2 - top) * C)
        total = l1 * w1 + l2 * w2
        mixed = acc[OWN] * (w1 / total) + racc[...] * (w2 / total)
        first = 256 * which
        obuf[first:first + mixed.shape[1]] = (jnp.transpose(mixed) * gates[which]).astype(jnp.bfloat16)

    my_main, my_shared = single_of(z, MAIN), single_of(z, SHARED)

    def out_main():
        merge(MAIN)
        to_all(lambda t: remote(
            obuf.at[rows(t * TOK, TOK)], outbuf.at[:, my_main], out_send, out_recv, z_dev(t)
        ).start())
        pltpu.make_async_copy(obuf.at[mine], outbuf.at[:, my_main], out_recv).start()

    def out_shared():
        merge(SHARED)

        def one(t):
            @pl.when(t // 8 == s)
            def _():
                remote(
                    obuf.at[rows(256 + lax.rem(t, 8) * TOK, TOK)], outbuf.at[:, my_shared],
                    out_send, out_recv, z_dev(t),
                ).start()

        to_all(one)

        @pl.when(zh == s)
        def _():
            pltpu.make_async_copy(
                obuf.at[rows(256 + zl * TOK, TOK)], outbuf.at[:, my_shared], out_recv
            ).start()

    def both(core, k):
        main_chunk(core, k)
        shared_chunk(core, k)

    def catch_up(i, carry):
        take(AHEAD + 1 + i, AHEAD + 1, EVEN + 1)

        def one(j, inner):
            whole(1 + 2 * i + j)
            return inner

        lax.fori_loop(0, 2, one, 0)
        return carry

    def keep_up(k, carry):
        take(k, EVEN + 1, RING)

        @pl.when(k == OWN_STEP)
        def _():
            own_ready(MAIN, 256)
            own_ready(SHARED, 128)
            both(OTHER, 0)
            for side in range(2):
                absorb(
                    acc_m, st_m, OWN, HALF[side], qa[OWN, HALF[side], q_cols[MAIN]], kv.at[MAIN, RING + side]
                )
            shared_chunk(OWN, RING + s)

        whole(k)
        return carry

    lax.fori_loop(0, EVEN - AHEAD, catch_up, 0)
    lax.fori_loop(EVEN + 1, RING, keep_up, 0)
    for which in range(2):
        for copy in partial(which):
            copy.start()
    out_main()
    out_shared()

    def sent(ref, sem):
        pltpu.make_async_copy(ref, ref, sem).wait()

    for which in range(2):
        sent(kv.at[which, 0, 0:240], kv_send.at[which])
        sent(kv.at[which, pl.ds(1, 15)], xy_send)

    @pl.when(zh == s)
    def _():
        sent(qa.at[0, 0:176], q_send)
        sent(obuf.at[pl.ds(0, 22 * TOK)], out_send)
        sent(kv.at[MAIN, 0], new_send)
        sent(kv.at[MAIN, 0, 0:96], new_send)

    @pl.when(zh != s)
    def _():
        sent(qa.at[0, 0:184], q_send)
        sent(obuf.at[pl.ds(0, 23 * TOK)], out_send)
        sent(kv.at[MAIN, 0], new_send)
        sent(kv.at[MAIN, 0, 0:112], new_send)

    pltpu.make_async_copy(outbuf, outbuf, out_recv).wait()
    out_ref[...] = outbuf[...]


def body(queries, keys_new, values_new, keys_old, values_old, gate_table, step_index):
    bf, f32 = jnp.bfloat16, jnp.float32
    dma = pltpu.SemaphoreType.DMA
    width = HEADS * HEAD_DIM
    return pl.pallas_call(
        kernel,
        out_shape=jax.ShapeDtypeStruct(queries.shape, bf),
        in_specs=[pl.BlockSpec(memory_space=pl.ANY)] * 6 + [pl.BlockSpec(memory_space=pltpu.SMEM)],
        out_specs=pl.BlockSpec(memory_space=pltpu.VMEM),
        scratch_shapes=[
            pltpu.VMEM((5, TOK, width), bf),
            pltpu.VMEM((2, TOK, 2 * width), bf),
            pltpu.VMEM((gate_table.shape[0], 256), f32),
            pltpu.VMEM((2, RING + 2, 256, 256), bf),
            pltpu.VMEM((2, 256, 256), bf),
            pltpu.VMEM((2, HEAD_DIM, 256), f32),
            pltpu.VMEM((2, HEAD_DIM, 128), f32),
            pltpu.VMEM((2, 8, 256), f32),
            pltpu.VMEM((2, 8, 128), f32),
            pltpu.VMEM((HEAD_DIM, 256), f32),
            pltpu.VMEM((HEAD_DIM, 128), f32),
            pltpu.VMEM((8, 256), f32),
            pltpu.VMEM((8, 128), f32),
            pltpu.VMEM((384, HEAD_DIM), bf),
            pltpu.VMEM((TOK, width), bf),
            dma((5,)), dma, dma((2,)), dma((2,)), dma, dma, dma((2,)), dma((2,)),
            dma, dma((2,)), dma((2, 2)), dma, dma((2, RING)), dma((2, 2)), dma((2, 2)), dma, dma,
        ],
        compiler_params=pltpu.CompilerParams(collective_id=0, has_side_effects=True),
    )(queries, keys_new, values_new, keys_old, values_old, gate_table, step_index)


def solution(mesh):
    tokens = P(("patch", "uly"), None)
    return jax.shard_map(
        body, mesh=mesh, in_specs=(tokens,) * 5 + (P(), P()), out_specs=tokens, check_vma=False
    )
```

```python
import jax
import jax.numpy as jnp
from jax import lax
from jax.experimental import pallas as pl
from jax.experimental.pallas import tpu as pltpu
from jax.sharding import PartitionSpec as P

HEADS = 24
HEAD_DIM = 128
MESH = pl.DeviceIdType.MESH
TOK = 16
RING = 16
SIDE = 4
C = HEAD_DIM ** (-0.5) * 1.4426950408889634

ORDER = (
    (0, 0), (1, 0), (3, 0), (0, 1), (0, 3), (2, 0), (1, 1), (1, 3),
    (3, 1), (3, 3), (0, 2), (2, 1), (2, 3), (1, 2), (3, 2), (2, 2),
)
SLOT = {pair: at for at, pair in enumerate(ORDER)}
HALF = (slice(0, 128), slice(128, 256))
QUARTER = (slice(0, 64), slice(64, 128))
MAIN, SHARED = 0, 1
OTHER, OWN = 0, 1
AHEAD, EVEN, LEAD = 3, 6, 3


def kernel(
    q_in, kn_in, vn_in, ko_in, vo_in, gate_in, step_ref, out_ref,
    raw, pairs, gbuf, km, ks, qm, qs, acc_m, acc_s, st_m, st_s, racc_m, racc_s, rst_m, rst_s, obuf, outbuf,
    stage_sem, gate_sem, kv_send, kv_recv, q_send, q_recv, qf_send, qf_recv,
    new_send, new_recv, old_sem, xy_send, xy_recv, part_send, part_recv, out_send, out_recv,
):
    p = lax.axis_index("patch")
    zl = lax.axis_index("uly")
    c = lax.rem(p, 2)
    y = lax.rem(p // 2, SIDE)
    zh = lax.rem(p // 8, 2)
    x = p // 16
    z = zh * 8 + zl
    g, s = z // 2, lax.rem(z, 2)

    def patch_of(x_, zh_, y_, c_):
        return ((x_ * 2 + zh_) * SIDE + y_) * 2 + c_

    def z_dev(z_):
        return {"patch": patch_of(x, z_ // 8, y, c), "uly": lax.rem(z_, 8)}

    def xy_dev(da, db):
        x_ = lax.rem(x + da * (1 - c) + db * c, SIDE)
        y_ = lax.rem(y + da * c + db * (1 - c), SIDE)
        return {"patch": patch_of(x_, zh, y_, c), "uly": zl}

    partner = {"patch": patch_of(x, zh, y, 1 - c), "uly": zl}
    beside = {"patch": patch_of(x, zh, y, c), "uly": zl + 1 - 2 * s}
    across = {"patch": patch_of(x, zh, y, 1 - c), "uly": zl + 1 - 2 * s}
    kv, qa = (km, ks), (qm, qs)

    def lanes(at, n=HEAD_DIM):
        return pl.ds(pl.multiple_of(at, HEAD_DIM), n)

    def rows(at, n):
        return pl.ds(pl.multiple_of(at, TOK), n)

    def remote(src, dst, ssem, rsem, dev):
        return pltpu.make_async_remote_copy(
            src_ref=src, dst_ref=dst, send_sem=ssem, recv_sem=rsem, device_id=dev, device_id_type=MESH
        )

    loads = [
        pltpu.make_async_copy(ref, raw.at[at], stage_sem.at[at])
        for at, ref in enumerate((ko_in, vo_in, kn_in, vn_in, q_in))
    ]
    for load in loads:
        load.start()
    gate_load = pltpu.make_async_copy(gate_in.at[:, lanes((3 * g + s) * HEAD_DIM, 256)], gbuf, gate_sem)
    gate_load.start()

    barrier = pltpu.get_barrier_semaphore()

    def greet(d, carry):
        pl.semaphore_signal(barrier, inc=1, device_id=z_dev(lax.rem(z + d, RING)), device_id_type=MESH)
        return carry

    lax.fori_loop(1, RING, greet, 0)
    for da, db in ((1, 0), (3, 0), (0, 1), (0, 3)):
        pl.semaphore_signal(barrier, inc=1, device_id=xy_dev(da, db), device_id_type=MESH)
    for dev in (partner, across):
        pl.semaphore_signal(barrier, inc=1, device_id=dev, device_id_type=MESH)
    for ref in (acc_m, acc_s):
        ref[...] = jnp.zeros_like(ref)
    for ref in (st_m, st_s):
        at = lax.broadcasted_iota(jnp.int32, ref.shape, 1)
        ref[...] = jnp.where(at == 0, -1e30, 0.0)
    for load in loads:
        load.wait()
    for at in range(4):
        for head in range(HEADS):
            col = (2 * head + at % 2) * HEAD_DIM
            pairs[at // 2, :, col:col + HEAD_DIM] = raw[at, :, head * HEAD_DIM:(head + 1) * HEAD_DIM]
    pl.semaphore_wait(barrier, RING - 1 + 4 + 2)

    mine, here = rows(z * TOK, TOK), rows(zl * TOK, TOK)

    def far(i):
        return lax.rem(z + 8 + ((i + 1) // 2) * (2 * lax.rem(i, 2) - 1), RING)

    def head_of(z_, which):
        group = 3 * (z_ // 2)
        return group + 1 if which == SHARED else group + 2 * lax.rem(z_, 2)

    def pair_of(z_, which):
        return lanes(256 * head_of(z_, which), 256)

    def single_of(z_, which):
        return lanes(HEAD_DIM * head_of(z_, which))

    def to_all(one):
        def step(i, carry):
            one(far(i))
            return carry

        lax.fori_loop(0, RING - 1, step, 0)

    def query_rows(z_):
        return rows(lax.rem(zh + z_, 2) * 128 + zl * TOK, TOK)

    def send_old_main(t):
        remote(
            pairs.at[0, :, pair_of(t, MAIN)], km.at[0, mine, :], kv_send.at[MAIN], kv_recv.at[MAIN], z_dev(t)
        ).start()

    def send_old_shared(t):
        @pl.when(lax.rem(t, 2) == zh)
        def _():
            remote(
                pairs.at[0, :, pair_of(t, SHARED)], ks.at[0, here, :],
                kv_send.at[SHARED], kv_recv.at[SHARED], z_dev(t),
            ).start()

    def send_q(t):
        remote(raw.at[4, :, single_of(t, MAIN)], qm.at[OWN, mine, :], q_send.at[MAIN], q_recv.at[MAIN], z_dev(t)).start()
        remote(
            raw.at[4, :, single_of(t, SHARED)], qs.at[OWN, query_rows(t), :],
            q_send.at[SHARED], q_recv.at[SHARED], z_dev(t),
        ).start()

    def send_new(t):
        remote(
            pairs.at[1, :, pair_of(t, MAIN)], km.at[RING + zh, mine, :],
            new_send.at[MAIN], new_recv.at[MAIN], z_dev(t),
        ).start()

    def send_new_shared(t):
        @pl.when(lax.rem(t, 2) == zh)
        def _():
            remote(
                pairs.at[1, :, pair_of(t, SHARED)], ks.at[RING, here, :],
                new_send.at[SHARED], new_recv.at[SHARED], z_dev(t),
            ).start()

    to_all(send_old_shared)
    to_all(send_old_main)
    pltpu.make_async_copy(pairs.at[0, :, pair_of(z, MAIN)], km.at[0, mine, :], kv_recv.at[MAIN]).start()

    @pl.when(s == zh)
    def _():
        pltpu.make_async_copy(
            pairs.at[0, :, pair_of(z, SHARED)], ks.at[0, here, :], kv_recv.at[SHARED]
        ).start()

    def start_queries():
        to_all(send_q)
        pltpu.make_async_copy(raw.at[4, :, single_of(z, MAIN)], qm.at[OWN, mine, :], q_recv.at[MAIN]).start()
        pltpu.make_async_copy(
            raw.at[4, :, single_of(z, SHARED)], qs.at[OWN, query_rows(z), :], q_recv.at[SHARED]
        ).start()

    def start_new():
        to_all(send_new_shared)
        to_all(send_new)
        pltpu.make_async_copy(
            pairs.at[1, :, pair_of(z, MAIN)], km.at[RING + zh, mine, :], new_recv.at[MAIN]
        ).start()

        @pl.when(s == zh)
        def _():
            pltpu.make_async_copy(
                pairs.at[1, :, pair_of(z, SHARED)], ks.at[RING, here, :], new_recv.at[SHARED]
            ).start()

    def push(which, src, dst, da, db, part=None):
        a, b = kv[which].at[SLOT[src]], kv[which].at[SLOT[dst]]
        if part is not None:
            piece = (HALF, QUARTER)[which][part]
            a, b = kv[which].at[SLOT[src], piece], kv[which].at[SLOT[dst], piece]
        remote(a, b, xy_send.at[which], xy_recv.at[which, SLOT[dst]], xy_dev(da, db)).start()

    def pass_on(which, pair):
        da, db = pair
        if pair == (0, 0):
            push(which, pair, (1, 0), 1, 0)
            push(which, pair, (3, 0), 3, 0)
        if pair == (1, 0):
            push(which, pair, (2, 0), 1, 0, 0)
        if pair == (3, 0):
            push(which, pair, (2, 0), 3, 0, 1)
        if db == 0:
            push(which, pair, (da, 1), 0, 1)
            push(which, pair, (da, 3), 0, 3)
        if db == 1:
            push(which, pair, (da, 2), 0, 1, 0)
        if db == 3:
            push(which, pair, (da, 2), 0, 3, 1)

    def begin(which):
        whole = kv[which].at[0]
        pltpu.make_async_copy(whole, whole, kv_recv.at[which]).wait()
        pass_on(which, (0, 0))

    def arrived(which, k):
        pltpu.make_async_copy(kv[which].at[k], kv[which].at[k], xy_recv.at[which, k]).wait()

    def take(which, k, first, last):
        arrived(which, k)
        for at in range(first, last):
            if ORDER[at][1] != 2:
                @pl.when(k == at)
                def _(pair=ORDER[at]):
                    pass_on(which, pair)

    begin(SHARED)
    begin(MAIN)
    start_queries()
    start_new()
    for side in range(2):
        keep = HALF[1 - side]
        pltpu.make_async_copy(km.at[0, keep], km.at[RING + side, keep], old_sem.at[side]).start()
    for k in range(1, AHEAD + LEAD + 1):
        for which, at in ((SHARED, k), (MAIN, k - LEAD)):
            if at >= 1:
                arrived(which, at)
                if ORDER[at][1] != 2:
                    pass_on(which, ORDER[at])

    for which in range(2):
        pltpu.make_async_copy(qa[which].at[OWN], qa[which].at[OWN], q_recv.at[which]).wait()
    over = [
        remote(qa[which].at[OWN], qa[which].at[OTHER], qf_send.at[which], qf_recv.at[which], partner)
        for which in range(2)
    ]
    for copy in over:
        copy.start()
    for copy in over:
        copy.wait()

    def absorb(jobs):
        scored, mixed = [], []
        for acc, st, at, queries, block in jobs:
            dots = lax.dot_general(
                block[:, :HEAD_DIM], queries, (((1,), (1,)), ((), ())), preferred_element_type=jnp.float32
            )
            core, cols = at
            scored.append((dots, jnp.maximum(st[core, 0:1, cols], jnp.max(dots, axis=0, keepdims=True))))
        for (acc, st, (core, cols), queries, block), (dots, new) in zip(jobs, scored):
            expo = jnp.exp2((dots - new) * C)
            shrink = jnp.exp2((st[core, 0:1, cols] - new) * C)
            mixed.append((shrink, jnp.sum(expo, axis=0, keepdims=True), lax.dot_general(
                block[:, HEAD_DIM:], expo.astype(jnp.bfloat16), (((0,), (0,)), ((), ())),
                preferred_element_type=jnp.float32,
            )))
        for (acc, st, (core, cols), queries, block), (dots, new), (shrink, added, update) in zip(
            jobs, scored, mixed
        ):
            st[core, 1:2, cols] = st[core, 1:2, cols] * shrink + added
            acc[core, :, cols] = acc[core, :, cols] * shrink + update
            st[core, 0:1, cols] = new

    full = slice(0, 256)

    def main_jobs(k, cores=(OTHER, OWN)):
        return [(acc_m, st_m, (core, full), qm[core], km.at[k]) for core in cores]

    def shared_jobs(k, cores=(OTHER, OWN)):
        return [(acc_s, st_s, (core, full), qs[core], ks.at[k]) for core in cores]

    def own_main():
        got = km.at[RING, 0:256]
        pltpu.make_async_copy(got, got, new_recv.at[MAIN]).wait()
        for side in range(2):
            keep = HALF[1 - side]
            pltpu.make_async_copy(km.at[0, keep], km.at[RING + side, keep], old_sem.at[side]).wait()
        absorb(main_jobs(0, (OTHER,)) + [
            (acc_m, st_m, (OWN, HALF[side]), qm[OWN, HALF[side]], km.at[RING + side]) for side in range(2)
        ])

    def own_shared():
        pltpu.make_async_copy(ks.at[RING], ks.at[RING], new_recv.at[SHARED]).wait()
        absorb(shared_jobs(0, (OTHER,)) + [
            (acc_s, st_s, (OWN, HALF[0]), qs[OWN, HALF[0]], ks.at[RING]),
            (acc_s, st_s, (OWN, HALF[1]), qs[OWN, HALF[1]], ks.at[0]),
        ])

    main_parts = [
        remote(acc_m.at[OTHER], racc_m, part_send.at[0], part_recv.at[0], partner),
        remote(st_m.at[OTHER], rst_m, part_send.at[1], part_recv.at[1], partner),
    ]
    shared_parts = []
    for at, (core, cols, dev) in enumerate(
        ((OWN, HALF[1], beside), (OTHER, HALF[1], across), (OTHER, HALF[0], partner))
    ):
        shared_parts += [
            remote(
                acc_s.at[core, :, cols], racc_s.at[at], part_send.at[2 + at], part_recv.at[2 + at], dev
            ),
            remote(st_s.at[core, :, cols], rst_s.at[at], part_send.at[5 + at], part_recv.at[5 + at], dev),
        ]

    gate_load.wait()
    picked = lax.broadcasted_iota(jnp.int32, gbuf.shape, 0) == step_ref[0]
    gate = jnp.sum(jnp.where(picked, gbuf[...], 0.0), axis=0, keepdims=True)
    gate_lo, gate_hi = gate[:, :HEAD_DIM], gate[:, HEAD_DIM:]
    gates = (jnp.where(s == 0, gate_lo, gate_hi), jnp.where(s == 0, gate_hi, gate_lo))

    def merge(terms):
        top = terms[0][0]
        for m, _, _ in terms[1:]:
            top = jnp.maximum(top, m)
        scales = [jnp.exp2((m - top) * C) for m, _, _ in terms]
        total = sum(l * w for (_, l, _), w in zip(terms, scales))
        return sum(a * (w / total) for (_, _, a), w in zip(terms, scales))

    def finish(which, mixed):
        first = 256 * which
        obuf[first:first + mixed.shape[1]] = (jnp.transpose(mixed) * gates[which]).astype(jnp.bfloat16)

    my_main, my_shared = single_of(z, MAIN), single_of(z, SHARED)

    def out_main():
        for copy in main_parts:
            copy.wait()
        finish(MAIN, merge([
            (st_m[OWN, 0:1], st_m[OWN, 1:2], acc_m[OWN]), (rst_m[0:1], rst_m[1:2], racc_m[...]),
        ]))
        to_all(lambda t: remote(
            obuf.at[rows(t * TOK, TOK)], outbuf.at[:, my_main], out_send, out_recv, z_dev(t)
        ).start())
        pltpu.make_async_copy(obuf.at[mine], outbuf.at[:, my_main], out_recv).start()

    def out_shared():
        for copy in shared_parts:
            copy.wait()
        home = HALF[0]
        finish(SHARED, merge(
            [(st_s[OWN, 0:1, home], st_s[OWN, 1:2, home], acc_s[OWN, :, home])]
            + [(rst_s[at, 0:1], rst_s[at, 1:2], racc_s[at]) for at in range(3)]
        ))

        def one(t):
            @pl.when(t // 8 == s)
            def _():
                remote(
                    obuf.at[rows(256 + lax.rem(t, 8) * TOK, TOK)], outbuf.at[:, my_shared],
                    out_send, out_recv, z_dev(t),
                ).start()

        to_all(one)

        @pl.when(zh == s)
        def _():
            pltpu.make_async_copy(
                obuf.at[rows(256 + zl * TOK, TOK)], outbuf.at[:, my_shared], out_recv
            ).start()

    def lead(k, carry):
        absorb(shared_jobs(k))
        return carry

    def catch_up(i, carry):
        k = AHEAD + 1 + i
        take(SHARED, k + LEAD, AHEAD + LEAD + 1, EVEN + LEAD + 1)
        take(MAIN, k, AHEAD + 1, EVEN + 1)

        def one(j, inner):
            absorb(main_jobs(1 + 2 * i + j) + shared_jobs(1 + 2 * i + j + LEAD))
            return inner

        lax.fori_loop(0, 2, one, 0)
        return carry

    def keep_up(k, carry):
        take(SHARED, k + LEAD, EVEN + LEAD + 1, RING)
        take(MAIN, k, EVEN + 1, RING - LEAD)
        absorb(main_jobs(k) + shared_jobs(k + LEAD))
        return carry

    def trail(k, carry):
        take(MAIN, k, RING - LEAD, RING)
        absorb(main_jobs(k))
        return carry

    lax.fori_loop(1, LEAD + 1, lead, 0)
    lax.fori_loop(0, EVEN - AHEAD, catch_up, 0)
    lax.fori_loop(EVEN + 1, RING - LEAD, keep_up, 0)
    own_shared()
    for copy in shared_parts:
        copy.start()
    lax.fori_loop(RING - LEAD, RING, trail, 0)
    own_main()
    for copy in main_parts:
        copy.start()
    out_main()
    out_shared()

    def sent(ref, sem):
        pltpu.make_async_copy(ref, ref, sem).wait()

    sent(km.at[0, 0:240], kv_send.at[MAIN])
    for which in range(2):
        sent(kv[which].at[pl.ds(1, 15)], xy_send.at[which])
        sent(qa[which].at[OWN, 0:240], q_send.at[which])
    sent(km.at[0, 0:240], new_send.at[MAIN])

    @pl.when(zh == s)
    def _():
        sent(ks.at[0, 0:112], kv_send.at[SHARED])
        sent(ks.at[0, 0:112], new_send.at[SHARED])
        sent(obuf.at[pl.ds(0, 22 * TOK)], out_send)

    @pl.when(zh != s)
    def _():
        sent(ks.at[0], kv_send.at[SHARED])
        sent(ks.at[0], new_send.at[SHARED])
        sent(obuf.at[pl.ds(0, 23 * TOK)], out_send)

    pltpu.make_async_copy(outbuf, outbuf, out_recv).wait()
    out_ref[...] = outbuf[...]


def body(queries, keys_new, values_new, keys_old, values_old, gate_table, step_index):
    bf, f32 = jnp.bfloat16, jnp.float32
    dma = pltpu.SemaphoreType.DMA
    width = HEADS * HEAD_DIM
    return pl.pallas_call(
        kernel,
        out_shape=jax.ShapeDtypeStruct(queries.shape, bf),
        in_specs=[pl.BlockSpec(memory_space=pl.ANY)] * 6 + [pl.BlockSpec(memory_space=pltpu.SMEM)],
        out_specs=pl.BlockSpec(memory_space=pltpu.VMEM),
        scratch_shapes=[
            pltpu.VMEM((5, TOK, width), bf),
            pltpu.VMEM((2, TOK, 2 * width), bf),
            pltpu.VMEM((gate_table.shape[0], 256), f32),
            pltpu.VMEM((RING + 2, 256, 256), bf),
            pltpu.VMEM((RING + 1, 128, 256), bf),
            pltpu.VMEM((2, 256, HEAD_DIM), bf),
            pltpu.VMEM((2, 256, HEAD_DIM), bf),
            pltpu.VMEM((2, HEAD_DIM, 256), f32),
            pltpu.VMEM((2, HEAD_DIM, 256), f32),
            pltpu.VMEM((2, 8, 256), f32),
            pltpu.VMEM((2, 8, 256), f32),
            pltpu.VMEM((HEAD_DIM, 256), f32),
            pltpu.VMEM((3, HEAD_DIM, 128), f32),
            pltpu.VMEM((8, 256), f32),
            pltpu.VMEM((3, 8, 128), f32),
            pltpu.VMEM((384, HEAD_DIM), bf),
            pltpu.VMEM((TOK, width), bf),
            dma((5,)), dma, dma((2,)), dma((2,)), dma((2,)), dma((2,)), dma((2,)), dma((2,)),
            dma((2,)), dma((2,)), dma((2,)), dma((2,)), dma((2, RING)), dma((8,)), dma((8,)), dma, dma,
        ],
        compiler_params=pltpu.CompilerParams(collective_id=0, has_side_effects=True),
    )(queries, keys_new, values_new, keys_old, values_old, gate_table, step_index)


def solution(mesh):
    tokens = P(("patch", "uly"), None)
    return jax.shard_map(
        body, mesh=mesh, in_specs=(tokens,) * 5 + (P(), P()), out_specs=tokens, check_vma=False
    )
```

```python
import jax
import jax.numpy as jnp
from jax import lax
from jax.experimental import pallas as pl
from jax.experimental.pallas import tpu as pltpu
from jax.sharding import PartitionSpec as P

HEADS = 24
HEAD_DIM = 128
MESH = pl.DeviceIdType.MESH
TOK = 16
RING = 16
SIDE = 4
C = HEAD_DIM ** (-0.5) * 1.4426950408889634

ORDER = (
    (0, 0), (1, 0), (3, 0), (0, 1), (0, 3), (2, 0), (1, 1), (1, 3),
    (3, 1), (3, 3), (0, 2), (2, 1), (2, 3), (1, 2), (3, 2), (2, 2),
)
SLOT = {pair: at for at, pair in enumerate(ORDER)}
HALF = (slice(0, 128), slice(128, 256))
QUARTER = (slice(0, 64), slice(64, 128))
MAIN, SHARED = 0, 1
OTHER, OWN = 0, 1
AHEAD, EVEN, LEAD = 3, 6, 3


def kernel(
    q_in, kn_in, vn_in, ko_in, vo_in, gate_in, step_ref, out_ref,
    raw, pairs, gbuf, km, ks, qm, qs, acc_m, acc_s, st_m, st_s, racc_m, racc_s, rst_m, rst_s, obuf, outbuf,
    stage_sem, gate_sem, kv_send, kv_recv, q_send, q_recv, qf_send, qf_recv,
    new_send, new_recv, old_sem, xy_send, xy_recv, part_send, part_recv, out_send, out_recv,
):
    p = lax.axis_index("patch")
    zl = lax.axis_index("uly")
    c = lax.rem(p, 2)
    y = lax.rem(p // 2, SIDE)
    zh = lax.rem(p // 8, 2)
    x = p // 16
    z = zh * 8 + zl
    g, s = z // 2, lax.rem(z, 2)

    def patch_of(x_, zh_, y_, c_):
        return ((x_ * 2 + zh_) * SIDE + y_) * 2 + c_

    def z_dev(z_):
        return {"patch": patch_of(x, z_ // 8, y, c), "uly": lax.rem(z_, 8)}

    def xy_dev(da, db):
        x_ = lax.rem(x + da * (1 - c) + db * c, SIDE)
        y_ = lax.rem(y + da * c + db * (1 - c), SIDE)
        return {"patch": patch_of(x_, zh, y_, c), "uly": zl}

    partner = {"patch": patch_of(x, zh, y, 1 - c), "uly": zl}
    beside = {"patch": patch_of(x, zh, y, c), "uly": zl + 1 - 2 * s}
    across = {"patch": patch_of(x, zh, y, 1 - c), "uly": zl + 1 - 2 * s}
    kv, qa = (km, ks), (qm, qs)

    def lanes(at, n=HEAD_DIM):
        return pl.ds(pl.multiple_of(at, HEAD_DIM), n)

    def rows(at, n):
        return pl.ds(pl.multiple_of(at, TOK), n)

    def remote(src, dst, ssem, rsem, dev):
        return pltpu.make_async_remote_copy(
            src_ref=src, dst_ref=dst, send_sem=ssem, recv_sem=rsem, device_id=dev, device_id_type=MESH
        )

    loads = [
        pltpu.make_async_copy(ref, raw.at[at], stage_sem.at[at])
        for at, ref in enumerate((ko_in, vo_in, kn_in, vn_in, q_in))
    ]
    for load in loads:
        load.start()
    gate_load = pltpu.make_async_copy(gate_in.at[:, lanes((3 * g + s) * HEAD_DIM, 256)], gbuf, gate_sem)
    gate_load.start()

    barrier = pltpu.get_barrier_semaphore()

    def greet(d, carry):
        pl.semaphore_signal(barrier, inc=1, device_id=z_dev(lax.rem(z + d, RING)), device_id_type=MESH)
        return carry

    lax.fori_loop(1, RING, greet, 0)
    for da, db in ((1, 0), (3, 0), (0, 1), (0, 3)):
        pl.semaphore_signal(barrier, inc=1, device_id=xy_dev(da, db), device_id_type=MESH)
    for dev in (partner, across):
        pl.semaphore_signal(barrier, inc=1, device_id=dev, device_id_type=MESH)
    for ref in (acc_m, acc_s):
        ref[...] = jnp.zeros_like(ref)
    for ref in (st_m, st_s):
        at = lax.broadcasted_iota(jnp.int32, ref.shape, 1)
        ref[...] = jnp.where(at == 0, -1e30, 0.0)
    for load in loads:
        load.wait()
    for at in range(4):
        for head in range(HEADS):
            col = (2 * head + at % 2) * HEAD_DIM
            pairs[at // 2, :, col:col + HEAD_DIM] = raw[at, :, head * HEAD_DIM:(head + 1) * HEAD_DIM]
    pl.semaphore_wait(barrier, RING - 1 + 4 + 2)

    mine, here = rows(z * TOK, TOK), rows(zl * TOK, TOK)

    def far(i):
        return lax.rem(z + 8 + ((i + 1) // 2) * (2 * lax.rem(i, 2) - 1), RING)

    def head_of(z_, which):
        group = 3 * (z_ // 2)
        return group + 1 if which == SHARED else group + 2 * lax.rem(z_, 2)

    def pair_of(z_, which):
        return lanes(256 * head_of(z_, which), 256)

    def single_of(z_, which):
        return lanes(HEAD_DIM * head_of(z_, which))

    def to_all(one):
        def step(i, carry):
            one(far(i))
            return carry

        lax.fori_loop(0, RING - 1, step, 0)

    def query_rows(z_):
        return rows(lax.rem(zh + z_, 2) * 128 + zl * TOK, TOK)

    def send_old_main(t):
        remote(
            pairs.at[0, :, pair_of(t, MAIN)], km.at[0, mine, :], kv_send.at[MAIN], kv_recv.at[MAIN], z_dev(t)
        ).start()

    def send_old_shared(t):
        @pl.when(lax.rem(t, 2) == zh)
        def _():
            remote(
                pairs.at[0, :, pair_of(t, SHARED)], ks.at[0, here, :],
                kv_send.at[SHARED], kv_recv.at[SHARED], z_dev(t),
            ).start()

    def send_q(t):
        remote(raw.at[4, :, single_of(t, MAIN)], qm.at[OWN, mine, :], q_send.at[MAIN], q_recv.at[MAIN], z_dev(t)).start()
        remote(
            raw.at[4, :, single_of(t, SHARED)], qs.at[OWN, query_rows(t), :],
            q_send.at[SHARED], q_recv.at[SHARED], z_dev(t),
        ).start()

    def send_new(t):
        remote(
            pairs.at[1, :, pair_of(t, MAIN)], km.at[RING + zh, mine, :],
            new_send.at[MAIN], new_recv.at[MAIN], z_dev(t),
        ).start()

    def send_new_shared(t):
        @pl.when(lax.rem(t, 2) == zh)
        def _():
            remote(
                pairs.at[1, :, pair_of(t, SHARED)], ks.at[RING, here, :],
                new_send.at[SHARED], new_recv.at[SHARED], z_dev(t),
            ).start()

    to_all(send_old_shared)
    to_all(send_old_main)
    pltpu.make_async_copy(pairs.at[0, :, pair_of(z, MAIN)], km.at[0, mine, :], kv_recv.at[MAIN]).start()

    @pl.when(s == zh)
    def _():
        pltpu.make_async_copy(
            pairs.at[0, :, pair_of(z, SHARED)], ks.at[0, here, :], kv_recv.at[SHARED]
        ).start()

    def start_queries():
        to_all(send_q)
        pltpu.make_async_copy(raw.at[4, :, single_of(z, MAIN)], qm.at[OWN, mine, :], q_recv.at[MAIN]).start()
        pltpu.make_async_copy(
            raw.at[4, :, single_of(z, SHARED)], qs.at[OWN, query_rows(z), :], q_recv.at[SHARED]
        ).start()

    def start_new():
        to_all(send_new_shared)
        to_all(send_new)
        pltpu.make_async_copy(
            pairs.at[1, :, pair_of(z, MAIN)], km.at[RING + zh, mine, :], new_recv.at[MAIN]
        ).start()

        @pl.when(s == zh)
        def _():
            pltpu.make_async_copy(
                pairs.at[1, :, pair_of(z, SHARED)], ks.at[RING, here, :], new_recv.at[SHARED]
            ).start()

    def push(which, src, dst, da, db, part=None):
        a, b = kv[which].at[SLOT[src]], kv[which].at[SLOT[dst]]
        if part is not None:
            piece = (HALF, QUARTER)[which][part]
            a, b = kv[which].at[SLOT[src], piece], kv[which].at[SLOT[dst], piece]
        remote(a, b, xy_send.at[which], xy_recv.at[which, SLOT[dst]], xy_dev(da, db)).start()

    def pass_on(which, pair):
        da, db = pair
        if pair == (0, 0):
            push(which, pair, (1, 0), 1, 0)
            push(which, pair, (3, 0), 3, 0)
        if pair == (1, 0):
            push(which, pair, (2, 0), 1, 0, 0)
        if pair == (3, 0):
            push(which, pair, (2, 0), 3, 0, 1)
        if db == 0:
            push(which, pair, (da, 1), 0, 1)
            push(which, pair, (da, 3), 0, 3)
        if db == 1:
            push(which, pair, (da, 2), 0, 1, 0)
        if db == 3:
            push(which, pair, (da, 2), 0, 3, 1)

    def begin(which):
        whole = kv[which].at[0]
        pltpu.make_async_copy(whole, whole, kv_recv.at[which]).wait()
        pass_on(which, (0, 0))

    def arrived(which, k):
        pltpu.make_async_copy(kv[which].at[k], kv[which].at[k], xy_recv.at[which, k]).wait()

    def take(which, k, first, last):
        arrived(which, k)
        for at in range(first, last):
            if ORDER[at][1] != 2:
                @pl.when(k == at)
                def _(pair=ORDER[at]):
                    pass_on(which, pair)

    begin(SHARED)
    begin(MAIN)
    start_queries()
    start_new()
    for side in range(2):
        keep = HALF[1 - side]
        pltpu.make_async_copy(km.at[0, keep], km.at[RING + side, keep], old_sem.at[side]).start()
    for k in range(1, AHEAD + LEAD + 1):
        for which, at in ((SHARED, k), (MAIN, k - LEAD)):
            if at >= 1:
                arrived(which, at)
                if ORDER[at][1] != 2:
                    pass_on(which, ORDER[at])

    for which in range(2):
        pltpu.make_async_copy(qa[which].at[OWN], qa[which].at[OWN], q_recv.at[which]).wait()
    over = [
        remote(qa[which].at[OWN], qa[which].at[OTHER], qf_send.at[which], qf_recv.at[which], partner)
        for which in range(2)
    ]
    for copy in over:
        copy.start()
    for copy in over:
        copy.wait()

    def absorb(jobs):
        scored, mixed = [], []
        for acc, st, (core, cols), queries, blocks in jobs:
            new, parts = st[core, 0:1, cols], []
            for block in blocks:
                dots = lax.dot_general(
                    block[:, :HEAD_DIM], queries, (((1,), (1,)), ((), ())),
                    preferred_element_type=jnp.float32,
                )
                new = jnp.maximum(new, jnp.max(dots, axis=0, keepdims=True))
                parts.append(dots)
            scored.append((parts, new))
        for (acc, st, (core, cols), queries, blocks), (parts, new) in zip(jobs, scored):
            shrink, added, update = jnp.exp2((st[core, 0:1, cols] - new) * C), 0.0, 0.0
            for block, dots in zip(blocks, parts):
                expo = jnp.exp2((dots - new) * C)
                added = added + jnp.sum(expo, axis=0, keepdims=True)
                update = update + lax.dot_general(
                    block[:, HEAD_DIM:], expo.astype(jnp.bfloat16), (((0,), (0,)), ((), ())),
                    preferred_element_type=jnp.float32,
                )
            mixed.append((shrink, added, update))
        for (acc, st, (core, cols), queries, blocks), (parts, new), (shrink, added, update) in zip(
            jobs, scored, mixed
        ):
            st[core, 1:2, cols] = st[core, 1:2, cols] * shrink + added
            acc[core, :, cols] = acc[core, :, cols] * shrink + update
            st[core, 0:1, cols] = new

    full = slice(0, 256)

    def main_jobs(*slots, cores=(OTHER, OWN)):
        return [(acc_m, st_m, (core, full), qm[core], [km.at[k] for k in slots]) for core in cores]

    def shared_jobs(*slots, cores=(OTHER, OWN)):
        return [(acc_s, st_s, (core, full), qs[core], [ks.at[k] for k in slots]) for core in cores]

    def own_main():
        got = km.at[RING, 0:256]
        pltpu.make_async_copy(got, got, new_recv.at[MAIN]).wait()
        for side in range(2):
            keep = HALF[1 - side]
            pltpu.make_async_copy(km.at[0, keep], km.at[RING + side, keep], old_sem.at[side]).wait()
        absorb(main_jobs(0, cores=(OTHER,)) + [
            (acc_m, st_m, (OWN, HALF[side]), qm[OWN, HALF[side]], [km.at[RING + side]]) for side in range(2)
        ])

    def own_shared():
        pltpu.make_async_copy(ks.at[RING], ks.at[RING], new_recv.at[SHARED]).wait()
        absorb(shared_jobs(0, cores=(OTHER,)) + [
            (acc_s, st_s, (OWN, HALF[0]), qs[OWN, HALF[0]], [ks.at[RING]]),
            (acc_s, st_s, (OWN, HALF[1]), qs[OWN, HALF[1]], [ks.at[0]]),
        ])

    main_parts = [
        remote(acc_m.at[OTHER], racc_m, part_send.at[0], part_recv.at[0], partner),
        remote(st_m.at[OTHER], rst_m, part_send.at[1], part_recv.at[1], partner),
    ]
    shared_parts = []
    for at, (core, cols, dev) in enumerate(
        ((OWN, HALF[1], beside), (OTHER, HALF[1], across), (OTHER, HALF[0], partner))
    ):
        shared_parts += [
            remote(
                acc_s.at[core, :, cols], racc_s.at[at], part_send.at[2 + at], part_recv.at[2 + at], dev
            ),
            remote(st_s.at[core, :, cols], rst_s.at[at], part_send.at[5 + at], part_recv.at[5 + at], dev),
        ]

    gate_load.wait()
    picked = lax.broadcasted_iota(jnp.int32, gbuf.shape, 0) == step_ref[0]
    gate = jnp.sum(jnp.where(picked, gbuf[...], 0.0), axis=0, keepdims=True)
    gate_lo, gate_hi = gate[:, :HEAD_DIM], gate[:, HEAD_DIM:]
    gates = (jnp.where(s == 0, gate_lo, gate_hi), jnp.where(s == 0, gate_hi, gate_lo))

    def merge(terms):
        top = terms[0][0]
        for m, _, _ in terms[1:]:
            top = jnp.maximum(top, m)
        scales = [jnp.exp2((m - top) * C) for m, _, _ in terms]
        total = sum(l * w for (_, l, _), w in zip(terms, scales))
        return sum(a * (w / total) for (_, _, a), w in zip(terms, scales))

    def finish(which, mixed):
        first = 256 * which
        obuf[first:first + mixed.shape[1]] = (jnp.transpose(mixed) * gates[which]).astype(jnp.bfloat16)

    my_main, my_shared = single_of(z, MAIN), single_of(z, SHARED)

    def out_main():
        for copy in main_parts:
            copy.wait()
        finish(MAIN, merge([
            (st_m[OWN, 0:1], st_m[OWN, 1:2], acc_m[OWN]), (rst_m[0:1], rst_m[1:2], racc_m[...]),
        ]))
        to_all(lambda t: remote(
            obuf.at[rows(t * TOK, TOK)], outbuf.at[:, my_main], out_send, out_recv, z_dev(t)
        ).start())
        pltpu.make_async_copy(obuf.at[mine], outbuf.at[:, my_main], out_recv).start()

    def out_shared():
        for copy in shared_parts:
            copy.wait()
        home = HALF[0]
        finish(SHARED, merge(
            [(st_s[OWN, 0:1, home], st_s[OWN, 1:2, home], acc_s[OWN, :, home])]
            + [(rst_s[at, 0:1], rst_s[at, 1:2], racc_s[at]) for at in range(3)]
        ))

        def one(t):
            @pl.when(t // 8 == s)
            def _():
                remote(
                    obuf.at[rows(256 + lax.rem(t, 8) * TOK, TOK)], outbuf.at[:, my_shared],
                    out_send, out_recv, z_dev(t),
                ).start()

        to_all(one)

        @pl.when(zh == s)
        def _():
            pltpu.make_async_copy(
                obuf.at[rows(256 + zl * TOK, TOK)], outbuf.at[:, my_shared], out_recv
            ).start()

    def catch_up(i, carry):
        k = AHEAD + 1 + i
        take(SHARED, k + LEAD, AHEAD + LEAD + 1, EVEN + LEAD + 1)
        take(MAIN, k, AHEAD + 1, EVEN + 1)

        at = 1 + 2 * i
        absorb(main_jobs(at, at + 1) + shared_jobs(at + LEAD, at + LEAD + 1))
        return carry

    def keep_up(k, carry):
        take(SHARED, k + LEAD, EVEN + LEAD + 1, RING)
        take(MAIN, k, EVEN + 1, RING - LEAD)
        absorb(main_jobs(k) + shared_jobs(k + LEAD))
        return carry

    def trail(k, carry):
        take(MAIN, k, RING - LEAD, RING)
        absorb(main_jobs(k))
        return carry

    absorb(shared_jobs(*range(1, LEAD + 1)))
    lax.fori_loop(0, EVEN - AHEAD, catch_up, 0)
    lax.fori_loop(EVEN + 1, RING - LEAD, keep_up, 0)
    own_shared()
    for copy in shared_parts:
        copy.start()
    lax.fori_loop(RING - LEAD, RING - 1, trail, 0)
    own_main()
    arrived(MAIN, RING - 1)
    absorb(main_jobs(RING - 1))
    for copy in main_parts:
        copy.start()
    out_main()
    out_shared()

    def sent(ref, sem):
        pltpu.make_async_copy(ref, ref, sem).wait()

    sent(km.at[0, 0:240], kv_send.at[MAIN])
    for which in range(2):
        sent(kv[which].at[pl.ds(1, 15)], xy_send.at[which])
        sent(qa[which].at[OWN, 0:240], q_send.at[which])
    sent(km.at[0, 0:240], new_send.at[MAIN])

    @pl.when(zh == s)
    def _():
        sent(ks.at[0, 0:112], kv_send.at[SHARED])
        sent(ks.at[0, 0:112], new_send.at[SHARED])
        sent(obuf.at[pl.ds(0, 22 * TOK)], out_send)

    @pl.when(zh != s)
    def _():
        sent(ks.at[0], kv_send.at[SHARED])
        sent(ks.at[0], new_send.at[SHARED])
        sent(obuf.at[pl.ds(0, 23 * TOK)], out_send)

    pltpu.make_async_copy(outbuf, outbuf, out_recv).wait()
    out_ref[...] = outbuf[...]


def body(queries, keys_new, values_new, keys_old, values_old, gate_table, step_index):
    bf, f32 = jnp.bfloat16, jnp.float32
    dma = pltpu.SemaphoreType.DMA
    width = HEADS * HEAD_DIM
    return pl.pallas_call(
        kernel,
        out_shape=jax.ShapeDtypeStruct(queries.shape, bf),
        in_specs=[pl.BlockSpec(memory_space=pl.ANY)] * 6 + [pl.BlockSpec(memory_space=pltpu.SMEM)],
        out_specs=pl.BlockSpec(memory_space=pltpu.VMEM),
        scratch_shapes=[
            pltpu.VMEM((5, TOK, width), bf),
            pltpu.VMEM((2, TOK, 2 * width), bf),
            pltpu.VMEM((gate_table.shape[0], 256), f32),
            pltpu.VMEM((RING + 2, 256, 256), bf),
            pltpu.VMEM((RING + 1, 128, 256), bf),
            pltpu.VMEM((2, 256, HEAD_DIM), bf),
            pltpu.VMEM((2, 256, HEAD_DIM), bf),
            pltpu.VMEM((2, HEAD_DIM, 256), f32),
            pltpu.VMEM((2, HEAD_DIM, 256), f32),
            pltpu.VMEM((2, 8, 256), f32),
            pltpu.VMEM((2, 8, 256), f32),
            pltpu.VMEM((HEAD_DIM, 256), f32),
            pltpu.VMEM((3, HEAD_DIM, 128), f32),
            pltpu.VMEM((8, 256), f32),
            pltpu.VMEM((3, 8, 128), f32),
            pltpu.VMEM((384, HEAD_DIM), bf),
            pltpu.VMEM((TOK, width), bf),
            dma((5,)), dma, dma((2,)), dma((2,)), dma((2,)), dma((2,)), dma((2,)), dma((2,)),
            dma((2,)), dma((2,)), dma((2,)), dma((2,)), dma((2, RING)), dma((8,)), dma((8,)), dma, dma,
        ],
        compiler_params=pltpu.CompilerParams(collective_id=0, has_side_effects=True),
    )(queries, keys_new, values_new, keys_old, values_old, gate_table, step_index)


def solution(mesh):
    tokens = P(("patch", "uly"), None)
    return jax.shard_map(
        body, mesh=mesh, in_specs=(tokens,) * 5 + (P(), P()), out_specs=tokens, check_vma=False
    )
```

```python
import jax
import jax.numpy as jnp
from jax import lax
from jax.experimental import pallas as pl
from jax.experimental.pallas import tpu as pltpu
from jax.sharding import PartitionSpec as P

HEADS = 24
HEAD_DIM = 128
MESH = pl.DeviceIdType.MESH
TOK = 16
RING = 16
SIDE = 4
C = HEAD_DIM ** (-0.5) * 1.4426950408889634

ORDER = (
    (0, 0), (1, 0), (3, 0), (0, 1), (0, 3), (2, 0), (1, 1), (1, 3),
    (3, 1), (3, 3), (0, 2), (2, 1), (2, 3), (1, 2), (3, 2), (2, 2),
)
SLOT = {pair: at for at, pair in enumerate(ORDER)}
HALF = (slice(0, 128), slice(128, 256))
QUARTER = (slice(0, 64), slice(64, 128))
MAIN, SHARED = 0, 1
OTHER, OWN = 0, 1
AHEAD, EVEN, LEAD = 3, 6, 3


def kernel(
    q_in, kn_in, vn_in, ko_in, vo_in, gate_in, step_ref, out_ref,
    raw, pairs, gbuf, km, ks, qm, qs, acc_m, acc_s, st_m, st_s, racc_m, racc_s, rst_m, rst_s, obuf, outbuf,
    stage_sem, gate_sem, kv_send, kv_recv, q_send, q_recv, qf_send, qf_recv,
    new_send, new_recv, old_sem, xy_send, xy_recv, part_send, part_recv, out_send, out_recv,
):
    p = lax.axis_index("patch")
    zl = lax.axis_index("uly")
    c = lax.rem(p, 2)
    y = lax.rem(p // 2, SIDE)
    zh = lax.rem(p // 8, 2)
    x = p // 16
    z = zh * 8 + zl
    g, s = z // 2, lax.rem(z, 2)

    def patch_of(x_, zh_, y_, c_):
        return ((x_ * 2 + zh_) * SIDE + y_) * 2 + c_

    def z_dev(z_):
        return {"patch": patch_of(x, z_ // 8, y, c), "uly": lax.rem(z_, 8)}

    def xy_dev(da, db):
        x_ = lax.rem(x + da * (1 - c) + db * c, SIDE)
        y_ = lax.rem(y + da * c + db * (1 - c), SIDE)
        return {"patch": patch_of(x_, zh, y_, c), "uly": zl}

    partner = {"patch": patch_of(x, zh, y, 1 - c), "uly": zl}
    beside = {"patch": patch_of(x, zh, y, c), "uly": zl + 1 - 2 * s}
    across = {"patch": patch_of(x, zh, y, 1 - c), "uly": zl + 1 - 2 * s}
    kv, qa = (km, ks), (qm, qs)

    def lanes(at, n=HEAD_DIM):
        return pl.ds(pl.multiple_of(at, HEAD_DIM), n)

    def rows(at, n):
        return pl.ds(pl.multiple_of(at, TOK), n)

    def remote(src, dst, ssem, rsem, dev):
        return pltpu.make_async_remote_copy(
            src_ref=src, dst_ref=dst, send_sem=ssem, recv_sem=rsem, device_id=dev, device_id_type=MESH
        )

    loads = [
        pltpu.make_async_copy(ref, raw.at[at], stage_sem.at[at])
        for at, ref in enumerate((ko_in, vo_in, kn_in, vn_in, q_in))
    ]
    for load in loads:
        load.start()
    gate_load = pltpu.make_async_copy(gate_in.at[:, lanes((3 * g + s) * HEAD_DIM, 256)], gbuf, gate_sem)
    gate_load.start()

    barrier = pltpu.get_barrier_semaphore()

    def greet(d, carry):
        pl.semaphore_signal(barrier, inc=1, device_id=z_dev(lax.rem(z + d, RING)), device_id_type=MESH)
        return carry

    lax.fori_loop(1, RING, greet, 0)
    for da, db in ((1, 0), (3, 0), (0, 1), (0, 3)):
        pl.semaphore_signal(barrier, inc=1, device_id=xy_dev(da, db), device_id_type=MESH)
    for dev in (partner, across):
        pl.semaphore_signal(barrier, inc=1, device_id=dev, device_id_type=MESH)
    for ref in (acc_m, acc_s):
        ref[...] = jnp.zeros_like(ref)
    for ref in (st_m, st_s):
        at = lax.broadcasted_iota(jnp.int32, ref.shape, 1)
        ref[...] = jnp.where(at == 0, -1e30, 0.0)
    for load in loads:
        load.wait()
    for at in range(4):
        for head in range(HEADS):
            col = (2 * head + at % 2) * HEAD_DIM
            pairs[at // 2, :, col:col + HEAD_DIM] = raw[at, :, head * HEAD_DIM:(head + 1) * HEAD_DIM]
    pl.semaphore_wait(barrier, RING - 1 + 4 + 2)

    mine, here = rows(z * TOK, TOK), rows(zl * TOK, TOK)

    def far(i):
        return lax.rem(z + 8 + ((i + 1) // 2) * (2 * lax.rem(i, 2) - 1), RING)

    def head_of(z_, which):
        group = 3 * (z_ // 2)
        return group + 1 if which == SHARED else group + 2 * lax.rem(z_, 2)

    def pair_of(z_, which):
        return lanes(256 * head_of(z_, which), 256)

    def single_of(z_, which):
        return lanes(HEAD_DIM * head_of(z_, which))

    def to_all(one):
        def step(i, carry):
            one(far(i))
            return carry

        lax.fori_loop(0, RING - 1, step, 0)

    def query_rows(z_):
        return rows(lax.rem(zh + z_, 2) * 128 + zl * TOK, TOK)

    def send_old_main(t):
        remote(
            pairs.at[0, :, pair_of(t, MAIN)], km.at[0, mine, :], kv_send.at[MAIN], kv_recv.at[MAIN], z_dev(t)
        ).start()

    def send_old_shared(t):
        @pl.when(lax.rem(t, 2) == zh)
        def _():
            remote(
                pairs.at[0, :, pair_of(t, SHARED)], ks.at[0, here, :],
                kv_send.at[SHARED], kv_recv.at[SHARED], z_dev(t),
            ).start()

    def send_q(t):
        remote(raw.at[4, :, single_of(t, MAIN)], qm.at[OWN, mine, :], q_send.at[MAIN], q_recv.at[MAIN], z_dev(t)).start()
        remote(
            raw.at[4, :, single_of(t, SHARED)], qs.at[OWN, query_rows(t), :],
            q_send.at[SHARED], q_recv.at[SHARED], z_dev(t),
        ).start()

    def send_new(t):
        remote(
            pairs.at[1, :, pair_of(t, MAIN)], km.at[RING + zh, mine, :],
            new_send.at[MAIN], new_recv.at[MAIN], z_dev(t),
        ).start()

    def send_new_shared(t):
        @pl.when(lax.rem(t, 2) == zh)
        def _():
            remote(
                pairs.at[1, :, pair_of(t, SHARED)], ks.at[RING, here, :],
                new_send.at[SHARED], new_recv.at[SHARED], z_dev(t),
            ).start()

    to_all(send_old_shared)
    to_all(send_old_main)
    pltpu.make_async_copy(pairs.at[0, :, pair_of(z, MAIN)], km.at[0, mine, :], kv_recv.at[MAIN]).start()

    @pl.when(s == zh)
    def _():
        pltpu.make_async_copy(
            pairs.at[0, :, pair_of(z, SHARED)], ks.at[0, here, :], kv_recv.at[SHARED]
        ).start()

    def start_queries():
        to_all(send_q)
        pltpu.make_async_copy(raw.at[4, :, single_of(z, MAIN)], qm.at[OWN, mine, :], q_recv.at[MAIN]).start()
        pltpu.make_async_copy(
            raw.at[4, :, single_of(z, SHARED)], qs.at[OWN, query_rows(z), :], q_recv.at[SHARED]
        ).start()

    def start_new():
        to_all(send_new_shared)
        to_all(send_new)
        pltpu.make_async_copy(
            pairs.at[1, :, pair_of(z, MAIN)], km.at[RING + zh, mine, :], new_recv.at[MAIN]
        ).start()

        @pl.when(s == zh)
        def _():
            pltpu.make_async_copy(
                pairs.at[1, :, pair_of(z, SHARED)], ks.at[RING, here, :], new_recv.at[SHARED]
            ).start()

    def push(which, src, dst, da, db, part=None):
        a, b = kv[which].at[SLOT[src]], kv[which].at[SLOT[dst]]
        if part is not None:
            piece = (HALF, QUARTER)[which][part]
            a, b = kv[which].at[SLOT[src], piece], kv[which].at[SLOT[dst], piece]
        remote(a, b, xy_send.at[which], xy_recv.at[which, SLOT[dst]], xy_dev(da, db)).start()

    def pass_on(which, pair):
        da, db = pair
        if pair == (0, 0):
            push(which, pair, (1, 0), 1, 0)
            push(which, pair, (3, 0), 3, 0)
        if pair == (1, 0):
            push(which, pair, (2, 0), 1, 0, 0)
        if pair == (3, 0):
            push(which, pair, (2, 0), 3, 0, 1)
        if db == 0:
            push(which, pair, (da, 1), 0, 1)
            push(which, pair, (da, 3), 0, 3)
        if db == 1:
            push(which, pair, (da, 2), 0, 1, 0)
        if db == 3:
            push(which, pair, (da, 2), 0, 3, 1)

    def begin(which):
        whole = kv[which].at[0]
        pltpu.make_async_copy(whole, whole, kv_recv.at[which]).wait()
        pass_on(which, (0, 0))

    def arrived(which, k):
        pltpu.make_async_copy(kv[which].at[k], kv[which].at[k], xy_recv.at[which, k]).wait()

    def take(which, k, first, last):
        arrived(which, k)
        for at in range(first, last):
            if ORDER[at][1] != 2:
                @pl.when(k == at)
                def _(pair=ORDER[at]):
                    pass_on(which, pair)

    begin(SHARED)
    begin(MAIN)
    start_queries()
    start_new()
    for side in range(2):
        keep = HALF[1 - side]
        pltpu.make_async_copy(km.at[0, keep], km.at[RING + side, keep], old_sem.at[side]).start()
    for k in range(1, AHEAD + LEAD + 1):
        for which, at in ((SHARED, k), (MAIN, k - LEAD)):
            if at >= 1:
                arrived(which, at)
                if ORDER[at][1] != 2:
                    pass_on(which, ORDER[at])

    for which in range(2):
        pltpu.make_async_copy(qa[which].at[OWN], qa[which].at[OWN], q_recv.at[which]).wait()
    over = [
        remote(qa[which].at[OWN], qa[which].at[OTHER], qf_send.at[which], qf_recv.at[which], partner)
        for which in range(2)
    ]
    for copy in over:
        copy.start()
    for copy in over:
        copy.wait()

    def absorb(jobs):
        scored, mixed = [], []
        for acc, st, (core, cols), queries, blocks in jobs:
            new, parts = st[core, 0:1, cols], []
            for block in blocks:
                dots = lax.dot_general(
                    block[:, :HEAD_DIM], queries, (((1,), (1,)), ((), ())),
                    preferred_element_type=jnp.float32,
                )
                new = jnp.maximum(new, jnp.max(dots, axis=0, keepdims=True))
                parts.append(dots)
            scored.append((parts, new))
        for (acc, st, (core, cols), queries, blocks), (parts, new) in zip(jobs, scored):
            shrink, added, update = jnp.exp2((st[core, 0:1, cols] - new) * C), 0.0, 0.0
            for block, dots in zip(blocks, parts):
                expo = jnp.exp2((dots - new) * C)
                added = added + jnp.sum(expo, axis=0, keepdims=True)
                update = update + lax.dot_general(
                    block[:, HEAD_DIM:], expo.astype(jnp.bfloat16), (((0,), (0,)), ((), ())),
                    preferred_element_type=jnp.float32,
                )
            mixed.append((shrink, added, update))
        for (acc, st, (core, cols), queries, blocks), (parts, new), (shrink, added, update) in zip(
            jobs, scored, mixed
        ):
            st[core, 1:2, cols] = st[core, 1:2, cols] * shrink + added
            acc[core, :, cols] = acc[core, :, cols] * shrink + update
            st[core, 0:1, cols] = new

    full = slice(0, 256)

    def main_jobs(*slots, cores=(OTHER, OWN)):
        return [(acc_m, st_m, (core, full), qm[core], [km.at[k] for k in slots]) for core in cores]

    def shared_jobs(*slots, cores=(OTHER, OWN)):
        return [(acc_s, st_s, (core, full), qs[core], [ks.at[k] for k in slots]) for core in cores]

    def own_main():
        got = km.at[RING, 0:256]
        pltpu.make_async_copy(got, got, new_recv.at[MAIN]).wait()
        for side in range(2):
            keep = HALF[1 - side]
            pltpu.make_async_copy(km.at[0, keep], km.at[RING + side, keep], old_sem.at[side]).wait()
        absorb(main_jobs(0, cores=(OTHER,)) + [
            (acc_m, st_m, (OWN, HALF[side]), qm[OWN, HALF[side]], [km.at[RING + side]]) for side in range(2)
        ])

    def own_shared():
        pltpu.make_async_copy(ks.at[RING], ks.at[RING], new_recv.at[SHARED]).wait()
        absorb(shared_jobs(0, cores=(OTHER,)) + [
            (acc_s, st_s, (OWN, HALF[0]), qs[OWN, HALF[0]], [ks.at[RING]]),
            (acc_s, st_s, (OWN, HALF[1]), qs[OWN, HALF[1]], [ks.at[0]]),
        ])

    main_parts = [
        remote(acc_m.at[OTHER], racc_m, part_send.at[0], part_recv.at[0], partner),
        remote(st_m.at[OTHER], rst_m, part_send.at[1], part_recv.at[1], partner),
    ]
    shared_parts = []
    for at, (core, cols, dev) in enumerate(
        ((OWN, HALF[1], beside), (OTHER, HALF[1], across), (OTHER, HALF[0], partner))
    ):
        shared_parts += [
            remote(
                acc_s.at[core, :, cols], racc_s.at[at], part_send.at[2 + at], part_recv.at[2 + at], dev
            ),
            remote(st_s.at[core, :, cols], rst_s.at[at], part_send.at[5 + at], part_recv.at[5 + at], dev),
        ]

    gate_load.wait()
    picked = lax.broadcasted_iota(jnp.int32, gbuf.shape, 0) == step_ref[0]
    gate = jnp.sum(jnp.where(picked, gbuf[...], 0.0), axis=0, keepdims=True)
    gate_lo, gate_hi = gate[:, :HEAD_DIM], gate[:, HEAD_DIM:]
    gates = (jnp.where(s == 0, gate_lo, gate_hi), jnp.where(s == 0, gate_hi, gate_lo))

    def merge(terms):
        top = terms[0][0]
        for m, _, _ in terms[1:]:
            top = jnp.maximum(top, m)
        scales = [jnp.exp2((m - top) * C) for m, _, _ in terms]
        total = sum(l * w for (_, l, _), w in zip(terms, scales))
        return sum(a * (w / total) for (_, _, a), w in zip(terms, scales))

    def finish(which, mixed):
        first = 256 * which
        obuf[first:first + mixed.shape[1]] = (jnp.transpose(mixed) * gates[which]).astype(jnp.bfloat16)

    my_main, my_shared = single_of(z, MAIN), single_of(z, SHARED)

    def out_main():
        for copy in main_parts:
            copy.wait()
        finish(MAIN, merge([
            (st_m[OWN, 0:1], st_m[OWN, 1:2], acc_m[OWN]), (rst_m[0:1], rst_m[1:2], racc_m[...]),
        ]))
        to_all(lambda t: remote(
            obuf.at[rows(t * TOK, TOK)], outbuf.at[:, my_main], out_send, out_recv, z_dev(t)
        ).start())
        pltpu.make_async_copy(obuf.at[mine], outbuf.at[:, my_main], out_recv).start()

    def out_shared():
        for copy in shared_parts:
            copy.wait()
        home = HALF[0]
        finish(SHARED, merge(
            [(st_s[OWN, 0:1, home], st_s[OWN, 1:2, home], acc_s[OWN, :, home])]
            + [(rst_s[at, 0:1], rst_s[at, 1:2], racc_s[at]) for at in range(3)]
        ))

        def one(t):
            @pl.when(t // 8 == s)
            def _():
                remote(
                    obuf.at[rows(256 + lax.rem(t, 8) * TOK, TOK)], outbuf.at[:, my_shared],
                    out_send, out_recv, z_dev(t),
                ).start()

        to_all(one)

        @pl.when(zh == s)
        def _():
            pltpu.make_async_copy(
                obuf.at[rows(256 + zl * TOK, TOK)], outbuf.at[:, my_shared], out_recv
            ).start()

    def catch_up(i, carry):
        k = AHEAD + 1 + i
        take(SHARED, k + LEAD, AHEAD + LEAD + 1, EVEN + LEAD + 1)
        take(MAIN, k, AHEAD + 1, EVEN + 1)

        at = 1 + 2 * i
        absorb(main_jobs(at, at + 1) + shared_jobs(at + LEAD, at + LEAD + 1))
        return carry

    def keep_up(k, carry):
        take(SHARED, k + LEAD, EVEN + LEAD + 1, RING)
        take(MAIN, k, EVEN + 1, RING - LEAD)
        absorb(main_jobs(k) + shared_jobs(k + LEAD))
        return carry

    def trail(k, carry):
        take(MAIN, k, RING - LEAD, RING)
        absorb(main_jobs(k))
        return carry

    absorb(shared_jobs(*range(1, LEAD + 1)))
    lax.fori_loop(0, EVEN - AHEAD, catch_up, 0)
    lax.fori_loop(EVEN + 1, RING - LEAD, keep_up, 0)
    own_shared()
    for copy in shared_parts:
        copy.start()
    lax.fori_loop(RING - LEAD, RING - 1, trail, 0)
    own_main()
    arrived(MAIN, RING - 1)
    absorb(main_jobs(RING - 1, cores=(OTHER,)))
    for copy in main_parts:
        copy.start()
    absorb(main_jobs(RING - 1, cores=(OWN,)))
    out_main()
    out_shared()

    def sent(ref, sem):
        pltpu.make_async_copy(ref, ref, sem).wait()

    sent(km.at[0, 0:240], kv_send.at[MAIN])
    for which in range(2):
        sent(kv[which].at[pl.ds(1, 15)], xy_send.at[which])
        sent(qa[which].at[OWN, 0:240], q_send.at[which])
    sent(km.at[0, 0:240], new_send.at[MAIN])

    @pl.when(zh == s)
    def _():
        sent(ks.at[0, 0:112], kv_send.at[SHARED])
        sent(ks.at[0, 0:112], new_send.at[SHARED])
        sent(obuf.at[pl.ds(0, 22 * TOK)], out_send)

    @pl.when(zh != s)
    def _():
        sent(ks.at[0], kv_send.at[SHARED])
        sent(ks.at[0], new_send.at[SHARED])
        sent(obuf.at[pl.ds(0, 23 * TOK)], out_send)

    pltpu.make_async_copy(outbuf, outbuf, out_recv).wait()
    out_ref[...] = outbuf[...]


def body(queries, keys_new, values_new, keys_old, values_old, gate_table, step_index):
    bf, f32 = jnp.bfloat16, jnp.float32
    dma = pltpu.SemaphoreType.DMA
    width = HEADS * HEAD_DIM
    return pl.pallas_call(
        kernel,
        out_shape=jax.ShapeDtypeStruct(queries.shape, bf),
        in_specs=[pl.BlockSpec(memory_space=pl.ANY)] * 6 + [pl.BlockSpec(memory_space=pltpu.SMEM)],
        out_specs=pl.BlockSpec(memory_space=pltpu.VMEM),
        scratch_shapes=[
            pltpu.VMEM((5, TOK, width), bf),
            pltpu.VMEM((2, TOK, 2 * width), bf),
            pltpu.VMEM((gate_table.shape[0], 256), f32),
            pltpu.VMEM((RING + 2, 256, 256), bf),
            pltpu.VMEM((RING + 1, 128, 256), bf),
            pltpu.VMEM((2, 256, HEAD_DIM), bf),
            pltpu.VMEM((2, 256, HEAD_DIM), bf),
            pltpu.VMEM((2, HEAD_DIM, 256), f32),
            pltpu.VMEM((2, HEAD_DIM, 256), f32),
            pltpu.VMEM((2, 8, 256), f32),
            pltpu.VMEM((2, 8, 256), f32),
            pltpu.VMEM((HEAD_DIM, 256), f32),
            pltpu.VMEM((3, HEAD_DIM, 128), f32),
            pltpu.VMEM((8, 256), f32),
            pltpu.VMEM((3, 8, 128), f32),
            pltpu.VMEM((384, HEAD_DIM), bf),
            pltpu.VMEM((TOK, width), bf),
            dma((5,)), dma, dma((2,)), dma((2,)), dma((2,)), dma((2,)), dma((2,)), dma((2,)),
            dma((2,)), dma((2,)), dma((2,)), dma((2,)), dma((2, RING)), dma((8,)), dma((8,)), dma, dma,
        ],
        compiler_params=pltpu.CompilerParams(collective_id=0, has_side_effects=True),
    )(queries, keys_new, values_new, keys_old, values_old, gate_table, step_index)


def solution(mesh):
    tokens = P(("patch", "uly"), None)
    return jax.shard_map(
        body, mesh=mesh, in_specs=(tokens,) * 5 + (P(), P()), out_specs=tokens, check_vma=False
    )
```
